256 devices in a mesh: seq: 64 (over z, x, core), tp: 4 (over y).
Axes of the slice: x: 4, y: 4, z: 8, core: 2. Of those that a mesh axis runs over, the one named last changes fastest.
Arguments:
- tokens: bfloat16 [8192, 2048], P('seq'), may hold values from -6 to 6
- input_heads: bfloat16 [8192, 4096], P('seq', 'tp'), may hold values from -6 to 6
- z_gate: bfloat16 [8192, 4096], P('seq', 'tp'), may hold values from -6 to 6
- b_proj: bfloat16 [8192, 128], P('seq'), may hold values from -0.5 to 0.5
- c_proj: bfloat16 [8192, 128], P('seq'), may hold values from -0.5 to 0.5
- step_size: float32 [8192, 64], P('seq', 'tp'), may hold values from 0.5 to 2
- decay_log: float32 [8192, 64], P('seq', 'tp'), as said below
- skip_gain: float32 [64], P('tp'), may hold values from 0.5 to 2
- init_state: float32 [64, 64, 128], P('tp'), may hold values from -48 to 48
- norm_gain: float32 [4096], P('tp'), may hold values from 0.1 to 1.9
- out_weight: bfloat16 [4096, 2048], P('tp'), may hold values from -0.09375 to 0.09375
- moe_gain: float32 [2048], replicated, may hold values from 0.1 to 1.9
- routes: int32 [8192, 2], P('seq'), may hold values from 0 to 63, all different within a row; in each aligned block of 128 rows (0 to 127, 128 to 255, ...) at most 8 rows name the same one
- route_weights: float32 [8192, 2], P('seq'), may hold values from 0.2 to 1
- w_gate: bfloat16 [64, 2048, 2048], P('seq', None, 'tp'), may hold values from -0.125 to 0.125
- w_up: bfloat16 [64, 2048, 2048], P('seq', None, 'tp'), may hold values from -0.125 to 0.125
- w_down: bfloat16 [64, 2048, 2048], P('seq', 'tp'), may hold values from -0.125 to 0.125
Outputs:
- mixed_out: bfloat16 [8192, 2048], P('seq', 'tp')
The draws below stay inside these ranges and needn't reach their ends.
Inputs may be any that keep to these rules, and one draw needn't show every extreme that they name: `decay_log`: every entry is negative. `routes`: the two experts of a row differ. In each aligned block of 128 rows (the rows of one device) no expert is named by more than 8 rows, a bound that some block reaches.
All inputs are finite; a program needn't handle non-finite values.
Results may differ from the reference program's by a relative error of at most 0.02.
Values may be sent and summed in bfloat16 or wider, within the bound.
A program may use at most 128 MiB of HBM per device.

```python
import math
import jax
import jax.numpy as jnp
import numpy as np
from jax import lax

D = 2048
SSM_CHANNEL_COUNT = 64
HDIM = 64
STATE = 128
FF = 2048
TOP = 2
TOK_DEV = 128
TOKENS = 8192
INNER = 4096
EXPERTS = 64
CAP = 512
SLOTS = 8
N_TP = 4


def draw_decay_log(key, part):
    derived_prng_keys = jax.random.split(jax.random.fold_in(key, 11), 10)
    blocks = TOKENS // TOK_DEV
    forget_count = SSM_CHANNEL_COUNT // 2
    forget_heads = jax.random.permutation(derived_prng_keys[0], SSM_CHANNEL_COUNT) < forget_count
    slow_rate = 0.2 / TOKENS * jax.random.uniform(derived_prng_keys[1], (SSM_CHANNEL_COUNT,), minval=0.1, maxval=1.0)
    block_factor = jnp.exp(jax.random.uniform(derived_prng_keys[2], (blocks, SSM_CHANNEL_COUNT), minval=math.log(0.5), maxval=math.log(2.0)))
    jitter = jax.random.uniform(derived_prng_keys[3], (TOKENS, SSM_CHANNEL_COUNT), minval=0.7, maxval=1.4)
    slow_vals = -slow_rate[None, :] * jnp.repeat(block_factor, TOK_DEV, axis=0) * jitter
    block_phase = jax.random.randint(derived_prng_keys[4], (SSM_CHANNEL_COUNT,), 0, 9)
    block_ids = jnp.arange(blocks, dtype=jnp.int32)
    fast_block = jnp.logical_and((block_ids[:, None] + block_phase[None, :]) % 9 == 0, forget_heads[None, :])
    late_kind = jax.random.randint(derived_prng_keys[5], (blocks, SSM_CHANNEL_COUNT), 0, 2) == 1
    fast_rate = jnp.exp(jax.random.uniform(derived_prng_keys[6], (blocks, SSM_CHANNEL_COUNT), minval=math.log(1.0 / 50.0), maxval=math.log(1.0 / 30.0)))
    late_total = jax.random.uniform(derived_prng_keys[7], (blocks, SSM_CHANNEL_COUNT), minval=2.0, maxval=6.0)
    late_length = max(1, TOK_DEV // 16)
    row_place = jnp.arange(TOKENS, dtype=jnp.int32) % TOK_DEV
    late_rows = (row_place >= TOK_DEV - late_length)[:, None]
    uniform_fast = -jnp.repeat(fast_rate, TOK_DEV, axis=0) * jitter
    late_fast = jnp.where(late_rows, -jnp.repeat(late_total, TOK_DEV, axis=0) / late_length * jitter, slow_vals)
    fast_vals = jnp.where(jnp.repeat(late_kind, TOK_DEV, axis=0), late_fast, uniform_fast)
    fading_rates = jnp.where(jnp.repeat(fast_block, TOK_DEV, axis=0), fast_vals, slow_vals)
    spots = jax.random.randint(derived_prng_keys[8], (2,), 0, TOKENS)
    surge_amplitude_grid = jnp.log(jax.random.uniform(derived_prng_keys[9], (2, SSM_CHANNEL_COUNT), minval=0.5, maxval=0.8))
    locus_flags = (jnp.arange(TOKENS)[:, None] == spots[None, :]).astype(jnp.float32)
    surge_amounts = jnp.sum(locus_flags[:, :, None] * surge_amplitude_grid[None, :, :], axis=1)
    return (fading_rates + surge_amounts).astype(jnp.float32)


def level_of(stream_key, shape, shards, low, top_value):
    level, own = 1.0, jax.random.fold_in(stream_key, 6)
    for dim, parts in shards:
        steps = jnp.exp(jax.random.uniform(jax.random.fold_in(own, dim), (parts,), jnp.float32, low / len(shards), top_value / len(shards)))
        level = level * jnp.repeat(steps, shape[dim] // parts).reshape([-1 if axis == dim else 1 for axis in range(len(shape))])
    return level


def deal_out(stream_key, own, number, rows, count, top, reach, skew):
    order = jax.random.permutation(stream_key, count)
    crowded, ordinary = shares(count, rows * top, reach, skew, True), shares(count, rows * top, reach, skew, False)
    places = jnp.arange(count)

    def named(tallies, rotation):
        used = int((tallies > 0).sum())
        fixed = max(1, used // 4)
        shifted = fixed + (places - fixed + rotation * (used - fixed)) % max(1, count - fixed)
        return jnp.zeros((count,), jnp.int32).at[order[jnp.where(places < fixed, places, shifted)]].set(jnp.asarray(tallies, jnp.int32))

    tallies = jnp.where(number % 4 == 0, named(crowded, number // 4), named(ordinary, number - number // 4 - 1))
    mixed = jax.random.permutation(jax.random.fold_in(own, 3), count)
    source_of, receiver = mixed[0:count // 2 * 2:2], mixed[1:count // 2 * 2:2]
    margin = jnp.minimum(tallies[source_of] - 1, reach - tallies[receiver]) // 2
    margin = jnp.where((source_of == order[0]) | (receiver == order[0]) | (tallies[receiver] == 0), 0, jnp.maximum(margin, 0))
    shifted = jax.random.randint(jax.random.fold_in(own, 4), (count // 2,), 0, 1 << 20) % (margin + 1)
    tallies = tallies.at[source_of].add(-shifted).at[receiver].add(shifted)
    items = jnp.searchsorted(jnp.cumsum(tallies), jnp.arange(rows * top), side="right").astype(jnp.int32)
    grid = items.reshape(top, rows).T
    grid = grid[jax.random.permutation(jax.random.fold_in(own, 1), rows)]
    rotation = jax.random.randint(jax.random.fold_in(own, 2), (rows, 1), 0, top)
    return jnp.take_along_axis(grid, (jnp.arange(top)[None, :] + rotation) % top, axis=1)


def shares(amount, total, reach, lean, full):
    loads = [(1 << 20) // math.isqrt(standing ** lean) + 1 for standing in range(1, amount + 1)]
    largest = reach if full else min(reach, max(-(-total // amount), total * loads[0] // sum(loads)))
    least = 1 if total - largest >= amount - 1 else 0
    counts, spare = [largest] + [least] * (amount - 1), total - largest - least * (amount - 1)
    while spare > 0:
        candidates = [i for i in range(1, amount) if counts[i] < largest] or [i for i in range(1, amount) if counts[i] < reach]
        mass, left = sum([loads[i] for i in candidates]), spare
        for i in candidates:
            more = min(reach - counts[i], max(1, left * loads[i] // mass), spare)
            counts[i] = counts[i] + more
            spare = spare - more
    return np.array(counts)


def scatter_about(key, dims, spread, most, cuts=(), held_as=jnp.bfloat16):
    result = jax.random.normal(key, dims, jnp.float32) * spread
    if len(cuts) > 0:
        result = level_of(key, dims, cuts, -0.22, 0.18) * result
    return jnp.clip(result, min=-most, max=most).astype(held_as)


def setup_inputs(seed: int = 0) -> dict:
    key_of = jax.random.split(jax.random.key(seed), 18)
    tokens = scatter_about(key_of[0], (TOKENS, D), 1.0, 6.0, ((0, 64),))
    input_heads = scatter_about(key_of[1], (TOKENS, INNER), 1.0, 6.0, ((0, 64), (1, 4)))
    z_gate = scatter_about(key_of[2], (TOKENS, INNER), 1.0, 6.0, ((0, 64), (1, 4)))
    b_proj = scatter_about(key_of[3], (TOKENS, STATE), STATE ** -0.5, 0.5, ((0, 64),))
    c_proj = scatter_about(key_of[4], (TOKENS, STATE), STATE ** -0.5, 0.5, ((0, 64),))
    step_size = jnp.clip(jnp.exp(math.log(2.0) - 1.3862944 * jax.random.uniform(key_of[5], (TOKENS, SSM_CHANNEL_COUNT), jnp.float32) ** level_of(key_of[5], (TOKENS, SSM_CHANNEL_COUNT), ((0, 64), (1, 4)), -0.2, 0.2)), 0.5, 2.0)
    decay_log = draw_decay_log(jax.random.fold_in(key_of[17], 71), 0)
    skip_gain = jnp.clip(0.5 + 1.5 * jax.random.uniform(key_of[7], (SSM_CHANNEL_COUNT,), jnp.float32) ** level_of(key_of[7], (SSM_CHANNEL_COUNT,), ((0, 4),), -0.2, 0.2), 0.5, 2.0)
    init_state = scatter_about(key_of[8], (SSM_CHANNEL_COUNT, HDIM, STATE), 8.0, 48.0, ((0, 4),), jnp.float32)
    norm_gain = jnp.clip(1.0 + 0.18 * jax.random.normal(key_of[9], (INNER,), jnp.float32), 0.1, 1.9)
    out_weight = scatter_about(key_of[10], (INNER, D), INNER ** -0.5, 0.09375, ((0, 4),))
    moe_gain = jnp.clip(1.0 + 0.18 * jax.random.normal(key_of[11], (D,), jnp.float32), 0.1, 1.9)
    routes_keys = jax.random.split(jax.random.fold_in(key_of[12], 1), TOKENS // TOK_DEV)
    routes_turns = jax.random.permutation(jax.random.fold_in(key_of[12], 3), TOKENS // TOK_DEV)
    routes = jax.vmap(lambda own, number: deal_out(jax.random.fold_in(key_of[12], 2), own, number, TOK_DEV, EXPERTS, TOP, SLOTS, 2))(routes_keys, routes_turns).reshape((TOKENS, TOP))
    route_weights = jnp.clip(0.2 + 0.8 * jax.random.uniform(key_of[13], (TOKENS, TOP), jnp.float32) ** level_of(key_of[13], (TOKENS, TOP), ((0, 64),), -0.2, 0.2), 0.2, 1.0)
    w_gate = scatter_about(key_of[14], (EXPERTS, D, FF), D ** -0.5, 0.125, ((0, 64), (2, 4)))
    w_up = scatter_about(key_of[15], (EXPERTS, D, FF), D ** -0.5, 0.125, ((0, 64), (2, 4)))
    w_down = scatter_about(key_of[16], (EXPERTS, FF, D), FF ** -0.5, 0.125, ((0, 64), (1, 4)))
    return dict(tokens=tokens, input_heads=input_heads, z_gate=z_gate, b_proj=b_proj, c_proj=c_proj, step_size=step_size, decay_log=decay_log, skip_gain=skip_gain, init_state=init_state, norm_gain=norm_gain, out_weight=out_weight, moe_gain=moe_gain, routes=routes, route_weights=route_weights, w_gate=w_gate, w_up=w_up, w_down=w_down)


def rms_rows(values, scale_gain):
    wide_vals = values.astype(jnp.float32)
    mean_sq = lax.optimization_barrier(jnp.mean(wide_vals * wide_vals, axis=-1, keepdims=True))
    return (wide_vals * lax.rsqrt(mean_sq + 1e-05) * scale_gain).astype(jnp.bfloat16)

def reference(tokens, input_heads, z_gate, b_proj, c_proj, step_size, decay_log, skip_gain, init_state, norm_gain, out_weight, moe_gain, routes, route_weights, w_gate, w_up, w_down):
    highest = lax.Precision.HIGHEST
    block_count = TOKENS // TOK_DEV
    x_blocks = input_heads.astype(jnp.float32).reshape(block_count, TOK_DEV, SSM_CHANNEL_COUNT, HDIM)
    b_blocks = b_proj.astype(jnp.float32).reshape(block_count, TOK_DEV, STATE)
    c_blocks = c_proj.astype(jnp.float32).reshape(block_count, TOK_DEV, STATE)
    step_blocks = step_size.reshape(block_count, TOK_DEV, SSM_CHANNEL_COUNT)
    log_blocks = decay_log.reshape(block_count, TOK_DEV, SSM_CHANNEL_COUNT)
    positions = jnp.arange(TOK_DEV, dtype=jnp.int32)
    causal = positions[:, None] >= positions[None, :]

    def span_step(state, pieces):
        x_block, b_block, c_block, step_block, log_block = pieces
        cum_decay = jnp.cumsum(log_block, axis=0)
        end_decay = cum_decay[-1]
        scores = jnp.einsum('in,jn->ij', c_block, b_block, precision=highest)
        cum_heads = cum_decay.T
        log_gap = cum_heads[:, :, None] - cum_heads[:, None, :]
        decay_mat = jnp.where(causal, jnp.exp(jnp.where(causal, log_gap, 0.0)), 0.0)
        mix_weights = decay_mat * scores[None] * step_block.T[:, None, :]
        intra_part = jnp.einsum('hij,jhp->ihp', mix_weights, x_block, precision=highest)
        inter_part = jnp.einsum('in,hpn->ihp', c_block, state, precision=highest) * jnp.exp(cum_decay)[:, :, None]
        weighted = (jnp.exp(end_decay[None, :] - cum_decay) * step_block)[:, :, None] * x_block
        new_state = jnp.exp(end_decay)[:, None, None] * state + jnp.einsum('jhp,jn->hpn', weighted, b_block, precision=highest)
        return (new_state, intra_part + inter_part)
    last_state, dual_scan_blocks = lax.scan(span_step, init_state, (x_blocks, b_blocks, c_blocks, step_blocks, log_blocks))
    x_wide = input_heads.astype(jnp.float32).reshape(TOKENS, SSM_CHANNEL_COUNT, HDIM)
    ssd_out = dual_scan_blocks.reshape(TOKENS, SSM_CHANNEL_COUNT, HDIM) + skip_gain[None, :, None] * x_wide
    z_wide = z_gate.astype(jnp.float32).reshape(TOKENS, SSM_CHANNEL_COUNT, HDIM)
    gated_vals = ssd_out * jax.nn.silu(z_wide)
    gated_vals = gated_vals * lax.rsqrt(lax.optimization_barrier(jnp.mean(gated_vals * gated_vals, axis=2, keepdims=True)) + 1e-05)
    normed = (gated_vals.reshape(TOKENS, INNER) * norm_gain).astype(jnp.bfloat16)
    projected = jnp.dot(normed, out_weight, preferred_element_type=jnp.float32)
    hidden = (tokens.astype(jnp.float32) + projected).astype(jnp.bfloat16)
    moe_in = rms_rows(hidden, moe_gain)
    flat_expert = routes.reshape(block_count, TOP * TOK_DEV).astype(jnp.int32)
    onehot = (flat_expert[:, :, None] == jnp.arange(EXPERTS, dtype=jnp.int32)[None, None, :]).astype(jnp.int32)
    earlier_count = (jnp.cumsum(onehot, axis=1) - onehot).astype(jnp.int32)
    slot_rank = lax.optimization_barrier(jnp.sum(earlier_count * onehot, axis=2)).astype(jnp.int32)
    block_base = (jnp.arange(block_count, dtype=jnp.int32) * SLOTS)[:, None]
    placed = (flat_expert * CAP + block_base + slot_rank).reshape(-1).astype(jnp.int32)
    owners = (jnp.arange(TOP * TOKENS, dtype=jnp.int32) // TOP).astype(jnp.int32)
    source = jnp.full((EXPERTS * CAP,), TOKENS, jnp.int32).at[placed].set(owners).reshape(EXPERTS, CAP)

    def expert_run(pieces):
        index_rows, gate_mat, up_mat, down_mat = pieces
        rows_in = jnp.take(moe_in, index_rows, axis=0, mode='fill', fill_value=0)
        gate_val = jnp.dot(rows_in, gate_mat, preferred_element_type=jnp.float32)
        up_val = jnp.dot(rows_in, up_mat, preferred_element_type=jnp.float32)
        act_vals = (jax.nn.silu(gate_val) * up_val).astype(jnp.bfloat16)
        act_groups = act_vals.astype(jnp.float32).reshape(CAP, N_TP, FF // N_TP)
        down_weight_groups = down_mat.astype(jnp.float32).reshape(N_TP, FF // N_TP, D)
        partials = jnp.einsum('rqf,qfd->qrd', act_groups, down_weight_groups, precision=highest)
        partials = partials.astype(jnp.bfloat16).astype(jnp.float32)
        return lax.optimization_barrier(jnp.sum(partials, axis=0)).astype(jnp.bfloat16)
    expert_outs = lax.map(expert_run, (source, w_gate, w_up, w_down))
    chosen_indices = jnp.take(expert_outs.reshape(EXPERTS * CAP, D), placed, axis=0).reshape(TOKENS, TOP, D)
    mixed_out = hidden.astype(jnp.float32) + lax.optimization_barrier(jnp.sum(route_weights[:, :, None] * chosen_indices.astype(jnp.float32), axis=1))
    return mixed_out.astype(jnp.bfloat16)
```

```python
import functools

import jax
import jax.numpy as jnp
from jax import lax
from jax.experimental import pallas as pl
from jax.experimental.pallas import tpu as pltpu
from jax.sharding import PartitionSpec as P

F32 = jnp.float32
BF16 = jnp.bfloat16
HI = lax.Precision.HIGHEST
MESH = pl.DeviceIdType.MESH
NZ, NX, NC = 8, 4, 2
NS = NZ * NX * NC
NY = 4
TOK = 128
HEADS = 16
INNER = 1024
WIDTH = 2048
SLICE = 512
SLOTS = 8
GROUPS = 4
GS = NS // GROUPS


def shifted(me, i, sign):
    z, x, c = me // 8, lax.rem(me // 2, 4), lax.rem(me, 2)
    dz, dx, dc = i // 8, lax.rem(i // 2, 4), lax.rem(i, 2)
    z2 = lax.rem(z + NZ + sign * dz, NZ)
    x2 = lax.rem(x + NX + sign * dx, NX)
    c2 = lax.rem(c + NC + sign * dc, NC)
    return z2 * 8 + x2 * 2 + c2


def iota(shape, dim):
    return lax.broadcasted_iota(jnp.int32, shape, dim)


def mm(a, b):
    return jnp.dot(a, b, preferred_element_type=F32)


def mm_nt(a, b, precision=None):
    return lax.dot_general(a, b, (((1,), (1,)), ((), ())), precision=precision, preferred_element_type=F32)


def split2(v):
    hi = v.astype(BF16)
    return hi, (v - hi.astype(F32)).astype(BF16)


def split3(v):
    hi, mid = split2(v)
    low = (v - hi.astype(F32) - mid.astype(F32)).astype(BF16)
    return hi, mid, low


def kernel(
    x_ref, z_ref, b_ref, c_ref, dt_ref, la_ref, skip_ref, ngain_ref, mgain_ref, routes_ref, rw_ref,
    tokens_hbm, init_hbm, wout_hbm, wg_hbm, wu_hbm, wd_hbm,
    out_ref,
    msg1, recv1, res, recv2, ybuf, szbuf, expcum, normed,
    tok_v, init_v, wout_v, wg_v, wu_v, wd_v,
    disp, xs, accg, accu, hid, wts,
    far_s, far_r, near_s, near_r, pbuf, rets, retr,
    wsem, s1, r1, s2, r2, sd, rd, sr, rr, ag_s, ag_r, rs_s, rs_r,
):
    me = lax.axis_index("seq")
    y = lax.axis_index("tp")
    up_y = lax.rem(y + 1, NY)
    dn_y = lax.rem(y + NY - 1, NY)
    far_y = lax.rem(y + 2, NY)

    barrier = pltpu.get_barrier_semaphore()

    def greet(i, carry):
        pl.semaphore_signal(barrier, inc=1, device_id=(shifted(me, i, 1), y), device_id_type=MESH)
        return carry

    lax.fori_loop(1, NS, greet, 0)
    for peer in (up_y, dn_y):
        pl.semaphore_signal(barrier, inc=1, device_id=(me, peer), device_id_type=MESH)

    own_col = pl.multiple_of(y * SLICE, SLICE)
    tile_row = pl.multiple_of((me // 8) * 128, 128)
    loads = [
        pltpu.make_async_copy(init_hbm.at[pl.ds(tile_row, 128), :], init_v, wsem.at[0]),
        pltpu.make_async_copy(tokens_hbm.at[:, pl.ds(own_col, SLICE)], tok_v, wsem.at[1]),
        pltpu.make_async_copy(wout_hbm, wout_v, wsem.at[2]),
        pltpu.make_async_copy(wg_hbm, wg_v, wsem.at[3]),
        pltpu.make_async_copy(wu_hbm, wu_v, wsem.at[4]),
        pltpu.make_async_copy(wd_hbm, wd_v, wsem.at[5]),
    ]
    for load in loads:
        load.start()

    rows = iota((TOK, TOK), 0)
    cols = iota((TOK, TOK), 1)
    causal = (rows >= cols).astype(F32)
    eye = (rows == cols).astype(BF16)
    dt = dt_ref[...]
    cum = jnp.dot(causal, la_ref[...], precision=HI, preferred_element_type=F32)
    end = cum[TOK - 1 : TOK, :]
    expand = (iota((HEADS, INNER), 1) // 64 == iota((HEADS, INNER), 0)).astype(BF16)
    w_hi, w_lo = split2(jnp.exp(end - cum) * dt)
    w_wide = mm(w_hi, expand) + mm(w_lo, expand)
    x_wide = x_ref[...].astype(F32)
    xw = (x_wide * w_wide).astype(BF16)
    d3 = split3(jnp.exp(end))
    k3 = split3(skip_ref[...])
    r8 = iota((8, HEADS), 0)
    small = jnp.zeros((8, HEADS), F32)
    for n, part in enumerate(d3 + k3):
        small = jnp.where(r8 == n, part.astype(F32), small)
    small_wide = mm(small.astype(BF16), expand)
    b_t = mm_nt(eye, b_ref[...]).astype(BF16)
    state_t = mm(b_t, xw)
    small_bf = small_wide.astype(BF16)
    for l in range(8):
        lanes = slice(l * 128, (l + 1) * 128)
        msg1[l * 8 : (l + 1) * 8, 0:16, :] = state_t[:, lanes].astype(BF16).reshape(8, 16, 128)
        msg1[l * 8 : (l + 1) * 8, 16:24, :] = jnp.broadcast_to(small_bf[None, :, lanes], (8, 8, 128))

    pl.semaphore_wait(barrier, NS - 1 + 2)

    def send1(i, carry):
        q = shifted(me, i, 1)
        pltpu.make_async_remote_copy(
            src_ref=msg1.at[q], dst_ref=recv1.at[me], send_sem=s1, recv_sem=r1,
            device_id=(q, y), device_id_type=MESH,
        ).start()
        return carry

    lax.fori_loop(1, NS, send1, 0)
    recv1[pl.ds(me, 1)] = msg1[pl.ds(me, 1)]

    e_hi, e_lo = split2(jnp.exp(cum))
    expcum[...] = mm(e_hi, expand) + mm(e_lo, expand)
    eye16 = (iota((HEADS, HEADS), 0) == iota((HEADS, HEADS), 1)).astype(F32)
    cum_t = mm_nt(eye16, cum, HI)
    dt_t = mm_nt(eye16, dt, HI)
    scores = mm_nt(c_ref[...], b_ref[...]) * causal
    low_half = (iota((TOK, 128), 1) < 64).astype(F32)
    skip_wide = small_wide[3:4, :] + small_wide[4:5, :] + small_wide[5:6, :]
    for l in range(8):
        lanes = slice(l * 128, (l + 1) * 128)
        mixes = []
        for h in (2 * l, 2 * l + 1):
            gap = jnp.minimum(cum[:, h : h + 1] - cum_t[h : h + 1, :], 0.0)
            mixes.append((jnp.exp(gap) * scores * dt_t[h : h + 1, :]).astype(BF16))
        x_l = x_wide[:, lanes]
        x_lo = x_l * low_half
        rhs = jnp.concatenate([x_lo.astype(BF16), (x_l - x_lo).astype(BF16)], axis=0)
        ybuf[:, lanes] = mm(jnp.concatenate(mixes, axis=1), rhs) + skip_wide[:, lanes] * x_l
        z_l = z_ref[:, lanes].astype(F32)
        szbuf[:, lanes] = 0.5 * z_l * (1.0 + jnp.tanh(0.5 * z_l))

    sel2 = (iota((8, 2), 0) == iota((8, 2), 1)).astype(F32)
    routes_t = mm_nt(sel2, routes_ref[...].astype(F32), HI).astype(jnp.int32)
    rw_t = mm_nt(sel2, rw_ref[...], HI)
    zme, xme, cme = me // 8, lax.rem(me // 2, 4), lax.rem(me, 2)
    off = (
        (((routes_t >> 3) - zme + 8) & 7) * 8
        + ((((routes_t >> 1) & 3) - xme + 4) & 3) * 2
        + (((routes_t & 1) - cme + 2) & 1)
    )
    place = iota((NS, TOK), 0)
    first = off[0:1, :] == place
    second = off[1:2, :] == place
    named = jnp.where(first, 1.0, 0.0) + jnp.where(second, 1.0, 0.0)
    weight = jnp.where(first, rw_t[0:1, :], 0.0) + jnp.where(second, rw_t[1:2, :], 0.0)
    before = (rows < cols).astype(BF16)
    rank = mm(named.astype(BF16), before)
    rank = jnp.where(named > 0.5, rank, -1.0)
    slot_id = iota((NS, SLOTS, TOK), 1).astype(F32)
    hit = jnp.broadcast_to(rank[:, None, :], (NS, SLOTS, TOK)) == slot_id
    pick = jnp.where(hit, 1.0, 0.0).reshape(NS * SLOTS, TOK).astype(BF16)
    pick_w = jnp.where(hit, jnp.broadcast_to(weight[:, None, :], (NS, SLOTS, TOK)), 0.0).reshape(NS * SLOTS, TOK)
    pw_hi, pw_lo = split2(pick_w)
    wts[0] = mm_nt(eye, pw_hi).astype(BF16)
    wts[1] = mm_nt(eye, pw_lo).astype(BF16)

    loads[0].wait()
    row0 = lax.rem(me, 8) * 16
    sel16 = (iota((16, 128), 1) == iota((16, 128), 0) + row0).astype(F32)
    start = mm_nt(sel16, init_v[...], HI)
    pltpu.make_async_remote_copy(
        src_ref=recv1.at[pl.ds(0, NS - 1)], dst_ref=recv1.at[pl.ds(0, NS - 1)], send_sem=s1, recv_sem=r1,
        device_id=(me, up_y), device_id_type=MESH,
    ).wait_recv()

    def step(p, state):
        res[p] = state.astype(BF16)
        piece = recv1[p].astype(F32)
        decay = piece[16:17, :] + piece[17:18, :] + piece[18:19, :]
        return decay * state + piece[0:16, :]

    lax.fori_loop(0, NS, step, start)

    def send2(i, carry):
        q = shifted(me, i, 1)
        pltpu.make_async_remote_copy(
            src_ref=res.at[q], dst_ref=recv2.at[me], send_sem=s2, recv_sem=r2,
            device_id=(q, y), device_id_type=MESH,
        ).start()
        return carry

    lax.fori_loop(1, NS, send2, 0)
    recv2[pl.ds(me, 1)] = res[pl.ds(me, 1)]
    pltpu.make_async_remote_copy(
        src_ref=recv2.at[pl.ds(0, NS - 1)], dst_ref=recv2.at[pl.ds(0, NS - 1)], send_sem=s2, recv_sem=r2,
        device_id=(me, up_y), device_id_type=MESH,
    ).wait_recv()

    same_head = (iota((128, 128), 0) // 64 == iota((128, 128), 1) // 64).astype(BF16)
    c_bf = c_ref[...]
    for l in range(8):
        lanes = slice(l * 128, (l + 1) * 128)
        entering = recv2[l * 8 : (l + 1) * 8].reshape(128, 128)
        v = ybuf[:, lanes] + mm(c_bf, entering) * expcum[:, lanes]
        v = v * szbuf[:, lanes]
        mean_sq = mm((v * v).astype(BF16), same_head) * (1.0 / 64.0)
        normed[:, lanes] = (v * lax.rsqrt(mean_sq + 1e-05) * ngain_ref[:, lanes]).astype(BF16)

    def rs_copy(n, k):
        sent, landed, side = (far_s, far_r, k) if k < 2 else (near_s, near_r, k - 2)
        return pltpu.make_async_remote_copy(
            src_ref=sent.at[n, side], dst_ref=landed.at[n, side],
            send_sem=rs_s.at[n, k], recv_sem=rs_r.at[n, k],
            device_id=(me, dn_y if side else up_y), device_id_type=MESH,
        )

    half = TOK // 2

    def rs_begin(n, lhs, w_v):
        part = mm(lhs, w_v[:, pl.ds(pl.multiple_of(far_y * SLICE, SLICE), SLICE)]).astype(BF16)
        far_s[n, 0] = part[:half]
        far_s[n, 1] = part[half:]
        rs_copy(n, 0).start()
        rs_copy(n, 1).start()
        for slot, where in ((0, up_y), (1, dn_y), (2, y)):
            pbuf[n, slot] = mm(lhs, w_v[:, pl.ds(pl.multiple_of(where * SLICE, SLICE), SLICE)])

    def rs_middle(n):
        rs_copy(n, 0).wait_recv()
        near_s[n, 0, :half] = (pbuf[n, 0, :half] + far_r[n, 0].astype(F32)).astype(BF16)
        near_s[n, 0, half:] = pbuf[n, 0, half:].astype(BF16)
        rs_copy(n, 2).start()
        rs_copy(n, 1).wait_recv()
        near_s[n, 1, :half] = pbuf[n, 1, :half].astype(BF16)
        near_s[n, 1, half:] = (pbuf[n, 1, half:] + far_r[n, 1].astype(F32)).astype(BF16)
        rs_copy(n, 3).start()

    def rs_end(n):
        rs_copy(n, 2).wait_recv()
        rs_copy(n, 3).wait_recv()
        return pbuf[n, 2] + near_r[n, 0].astype(F32) + near_r[n, 1].astype(F32)

    loads[2].wait()
    rs_begin(GROUPS, normed[...], wout_v)
    loads[1].wait()
    rs_middle(GROUPS)
    hidden = (tok_v[...].astype(F32) + rs_end(GROUPS)).astype(BF16)
    hid[...] = hidden
    disp[...] = mm(pick, hidden).astype(BF16).reshape(NS, SLOTS, SLICE)

    for g in range(GROUPS):
        def send_d(i, carry):
            pltpu.make_async_remote_copy(
                src_ref=disp.at[i], dst_ref=xs.at[0, i], send_sem=sd, recv_sem=rd.at[g],
                device_id=(shifted(me, i, 1), y), device_id_type=MESH,
            ).start()
            return carry

        lax.fori_loop(max(1, g * GS), (g + 1) * GS, send_d, 0)
    xs[0, 0] = disp[0]
    for load in loads[3:]:
        load.wait()

    def ag_copy(g, k):
        src, dst, first, count, peer = (
            (0, 1, 0, GS, up_y),
            (0, 3, 0, GS, dn_y),
            (1, 2, 0, GS // 2, up_y),
            (3, 2, GS // 2, GS // 2, dn_y),
        )[k]
        part = pl.ds(g * GS + first, count)
        return pltpu.make_async_remote_copy(
            src_ref=xs.at[src, part], dst_ref=xs.at[dst, part],
            send_sem=ag_s.at[g, k], recv_sem=ag_r.at[g, k], device_id=(me, peer), device_id_type=MESH,
        )

    def arrive(g):
        count = GS - 1 if g == 0 else GS
        part = xs.at[0, pl.ds((g + 1) * GS - count, count)]
        pltpu.make_async_remote_copy(
            src_ref=part, dst_ref=part, send_sem=sd, recv_sem=rd.at[g], device_id=(me, up_y), device_id_type=MESH,
        ).wait_recv()
        ag_copy(g, 0).start()
        ag_copy(g, 1).start()

    def forward(g):
        ag_copy(g, 0).wait_recv()
        ag_copy(g, 2).start()
        ag_copy(g, 1).wait_recv()
        ag_copy(g, 3).start()

    def expert(g):
        ag_copy(g, 2).wait_recv()
        ag_copy(g, 3).wait_recv()
        accg[...] = jnp.zeros_like(accg)
        accu[...] = jnp.zeros_like(accu)

        def piece(o, total):
            owner = lax.rem(y + NY - o, NY)
            at = pl.multiple_of(owner * SLICE, SLICE)
            v = xs[o, pl.ds(g * GS, GS)].astype(F32).reshape(TOK, SLICE)
            vg = (v * mgain_ref[:, pl.ds(at, SLICE)]).astype(BF16)
            accg[...] += mm(vg, wg_v[pl.ds(at, SLICE), :])
            accu[...] += mm(vg, wu_v[pl.ds(at, SLICE), :])
            return total + jnp.sum(v * v, axis=1, keepdims=True)

        total = lax.fori_loop(0, NY, piece, jnp.zeros((TOK, 1), F32))
        scale = lax.rsqrt(total * (1.0 / WIDTH) + 1e-05)
        gate = accg[...] * scale
        act = (0.5 * gate * (1.0 + jnp.tanh(0.5 * gate)) * (accu[...] * scale)).astype(BF16)
        rs_begin(g, act, wd_v)

    def give_back(g):
        rets[g * GS : (g + 1) * GS] = rs_end(g).astype(BF16).reshape(GS, SLOTS, SLICE)

        def send_r(i, carry):
            pltpu.make_async_remote_copy(
                src_ref=rets.at[i], dst_ref=retr.at[i], send_sem=sr, recv_sem=rr.at[g],
                device_id=(shifted(me, i, -1), y), device_id_type=MESH,
            ).start()
            return carry

        lax.fori_loop(max(1, g * GS), (g + 1) * GS, send_r, 0)

    stages = (arrive, forward, expert, rs_middle, give_back)
    for k in range(GROUPS + len(stages) - 1):
        for n, stage in enumerate(stages):
            if 0 <= k - n < GROUPS:
                stage(k - n)

    retr[0] = rets[0]
    total = hid[...].astype(F32)
    for g in range(GROUPS):
        count = GS - 1 if g == 0 else GS
        part = retr.at[pl.ds((g + 1) * GS - count, count)]
        pltpu.make_async_remote_copy(
            src_ref=part, dst_ref=part, send_sem=sr, recv_sem=rr.at[g], device_id=(me, up_y), device_id_type=MESH,
        ).wait_recv()
        back = retr[g * GS : (g + 1) * GS].reshape(TOK, SLICE)
        lanes = slice(g * TOK, (g + 1) * TOK)
        total = total + mm(wts[0, :, lanes], back) + mm(wts[1, :, lanes], back)
    out_ref[...] = total.astype(BF16)

    for buf, sem in ((msg1, s1), (res, s2), (disp, sd), (rets, sr)):
        part = buf.at[pl.ds(0, NS - 1)]
        pltpu.make_async_remote_copy(
            src_ref=part, dst_ref=part, send_sem=sem, recv_sem=r1, device_id=(me, up_y), device_id_type=MESH,
        ).wait_send()
    for g in range(GROUPS):
        for k in range(4):
            ag_copy(g, k).wait_send()
    for n in range(GROUPS + 1):
        for k in range(4):
            rs_copy(n, k).wait_send()


def body(
    tokens, input_heads, z_gate, b_proj, c_proj, step_size, decay_log, skip_gain, init_state, norm_gain,
    out_weight, moe_gain, routes, route_weights, w_gate, w_up, w_down,
):
    vmem = pl.BlockSpec(memory_space=pltpu.VMEM)
    hbm = pl.BlockSpec(memory_space=pl.ANY)
    dma = pltpu.SemaphoreType.DMA
    n = GROUPS + 1
    scratch = [
        pltpu.VMEM((NS, 24, 128), BF16),
        pltpu.VMEM((NS, 24, 128), BF16),
        pltpu.VMEM((NS, 16, 128), BF16),
        pltpu.VMEM((NS, 16, 128), BF16),
        pltpu.VMEM((TOK, INNER), F32),
        pltpu.VMEM((TOK, INNER), F32),
        pltpu.VMEM((TOK, INNER), F32),
        pltpu.VMEM((TOK, INNER), BF16),
        pltpu.VMEM((TOK, SLICE), BF16),
        pltpu.VMEM((128, 128), F32),
        pltpu.VMEM((INNER, WIDTH), BF16),
        pltpu.VMEM((WIDTH, SLICE), BF16),
        pltpu.VMEM((WIDTH, SLICE), BF16),
        pltpu.VMEM((SLICE, WIDTH), BF16),
        pltpu.VMEM((NS, SLOTS, SLICE), BF16),
        pltpu.VMEM((NY, NS, SLOTS, SLICE), BF16),
        pltpu.VMEM((TOK, SLICE), F32),
        pltpu.VMEM((TOK, SLICE), F32),
        pltpu.VMEM((TOK, SLICE), BF16),
        pltpu.VMEM((2, TOK, NS * SLOTS), BF16),
        pltpu.VMEM((n, 2, TOK // 2, SLICE), BF16),
        pltpu.VMEM((n, 2, TOK // 2, SLICE), BF16),
        pltpu.VMEM((n, 2, TOK, SLICE), BF16),
        pltpu.VMEM((n, 2, TOK, SLICE), BF16),
        pltpu.VMEM((n, 3, TOK, SLICE), F32),
        pltpu.VMEM((NS, SLOTS, SLICE), BF16),
        pltpu.VMEM((NS, SLOTS, SLICE), BF16),
        dma((6,)),
        dma, dma, dma, dma,
        dma, dma((GROUPS,)),
        dma, dma((GROUPS,)),
        dma((GROUPS, 4)), dma((GROUPS, 4)),
        dma((n, 4)), dma((n, 4)),
    ]
    return pl.pallas_call(
        kernel,
        out_shape=jax.ShapeDtypeStruct((TOK, SLICE), BF16),
        in_specs=[vmem] * 11 + [hbm] * 6,
        out_specs=vmem,
        scratch_shapes=scratch,
        name="mixer_moe",
        compiler_params=pltpu.CompilerParams(
            collective_id=0, has_side_effects=True, vmem_limit_bytes=56 * 1024 * 1024
        ),
    )(
        input_heads, z_gate, b_proj, c_proj, step_size, decay_log, skip_gain.reshape(1, HEADS),
        norm_gain.reshape(1, INNER), moe_gain.reshape(1, WIDTH), routes, route_weights,
        tokens, init_state.reshape(INNER, 128), out_weight, w_gate[0], w_up[0], w_down[0],
    )


def solution(mesh):
    in_specs = (
        P("seq", None),
        P("seq", "tp"),
        P("seq", "tp"),
        P("seq", None),
        P("seq", None),
        P("seq", "tp"),
        P("seq", "tp"),
        P("tp"),
        P("tp", None, None),
        P("tp"),
        P("tp", None),
        P(),
        P("seq", None),
        P("seq", None),
        P("seq", None, "tp"),
        P("seq", None, "tp"),
        P("seq", "tp", None),
    )
    return jax.shard_map(body, mesh=mesh, in_specs=in_specs, out_specs=P("seq", "tp"), check_vma=False)
```

```python
import functools

import jax
import jax.numpy as jnp
from jax import lax
from jax.experimental import pallas as pl
from jax.experimental.pallas import tpu as pltpu
from jax.sharding import PartitionSpec as P

F32 = jnp.float32
BF16 = jnp.bfloat16
HI = lax.Precision.HIGHEST
MESH = pl.DeviceIdType.MESH
NZ, NX, NC = 8, 4, 2
NS = NZ * NX * NC
NP = NX * NC
NY = 4
TOK = 128
HEADS = 16
INNER = 1024
WIDTH = 2048
SLICE = 512
SLOTS = 8
GROUPS = 4
GS = NS // GROUPS
DZ = (1, 7, 2, 6, 0, 4, 3, 5)
OWN = DZ.index(0) * NP


def shifted(me, i, sign):
    z, x, c = me // 8, lax.rem(me // 2, 4), lax.rem(me, 2)
    dz, dx, dc = i // 8, lax.rem(i // 2, 4), lax.rem(i, 2)
    z2 = lax.rem(z + NZ + sign * dz, NZ)
    x2 = lax.rem(x + NX + sign * dx, NX)
    c2 = lax.rem(c + NC + sign * dc, NC)
    return z2 * 8 + x2 * 2 + c2


def iota(shape, dim):
    return lax.broadcasted_iota(jnp.int32, shape, dim)


def mm(a, b):
    return jnp.dot(a, b, preferred_element_type=F32)


def mm_nt(a, b, precision=None):
    return lax.dot_general(a, b, (((1,), (1,)), ((), ())), precision=precision, preferred_element_type=F32)


def split2(v):
    hi = v.astype(BF16)
    return hi, (v - hi.astype(F32)).astype(BF16)


def split3(v):
    hi, mid = split2(v)
    low = (v - hi.astype(F32) - mid.astype(F32)).astype(BF16)
    return hi, mid, low


def kernel(
    x_ref, z_ref, b_ref, c_ref, dt_ref, la_ref, skip_ref, ngain_ref, mgain_ref, routes_ref, rw_ref,
    tokens_hbm, init_hbm, wout_hbm, wg_hbm, wu_hbm, wd_hbm,
    out_ref,
    msg1, recv1, msg2, recv2, msg3, recv3, msg4, recv4, inner, through, ybuf, szbuf, expcum, normed,
    tok_v, init_v, wout_v, wg_v, wu_v, wd_v,
    disp, xs, accg, accu, hid, wts,
    far_s, far_r, near_s, near_r, pbuf, rets, retr,
    wsem, xsem_s, xsem_r, sd, rd, sr, rr, ag_s, ag_r, rs_s, rs_r,
):
    me = lax.axis_index("seq")
    y = lax.axis_index("tp")
    up_y = lax.rem(y + 1, NY)
    dn_y = lax.rem(y + NY - 1, NY)
    far_y = lax.rem(y + 2, NY)

    barrier = pltpu.get_barrier_semaphore()

    def greet(i, carry):
        pl.semaphore_signal(barrier, inc=1, device_id=(shifted(me, i, 1), y), device_id_type=MESH)
        return carry

    lax.fori_loop(1, NP, greet, 0)
    lax.fori_loop(1, NZ, lambda i, carry: greet(i * NP, carry), 0)
    for peer in (up_y, dn_y):
        pl.semaphore_signal(barrier, inc=1, device_id=(me, peer), device_id_type=MESH)

    own_col = pl.multiple_of(y * SLICE, SLICE)
    plane, spot = me // NP, lax.rem(me, NP)
    tile_row = pl.multiple_of(spot * 128, 128)
    loads = [
        pltpu.make_async_copy(init_hbm.at[pl.ds(tile_row, 128), :], init_v, wsem.at[0]),
        pltpu.make_async_copy(tokens_hbm.at[:, pl.ds(own_col, SLICE)], tok_v, wsem.at[1]),
        pltpu.make_async_copy(wout_hbm, wout_v, wsem.at[2]),
        pltpu.make_async_copy(wg_hbm, wg_v, wsem.at[3]),
        pltpu.make_async_copy(wu_hbm, wu_v, wsem.at[4]),
        pltpu.make_async_copy(wd_hbm, wd_v, wsem.at[5]),
    ]
    for load in loads:
        load.start()

    rows = iota((TOK, TOK), 0)
    cols = iota((TOK, TOK), 1)
    causal = (rows >= cols).astype(F32)
    eye = (rows == cols).astype(BF16)
    eye_f = eye.astype(F32)
    dt_t = dt_ref[...]
    cum_t = mm_nt(la_ref[...], causal, HI)
    cum = mm_nt(eye_f, cum_t, HI)
    dt = mm_nt(eye_f, dt_t, HI)
    end = cum[TOK - 1 : TOK, :]
    expand = (iota((HEADS, INNER), 1) // 64 == iota((HEADS, INNER), 0)).astype(BF16)
    w_hi, w_lo = split2(jnp.exp(end - cum) * dt)
    w_wide = mm(w_hi, expand) + mm(w_lo, expand)
    x_wide = x_ref[...].astype(F32)
    xw = (x_wide * w_wide).astype(BF16)
    d3 = split3(jnp.exp(end))
    k3 = split3(skip_ref[...])
    r8 = iota((8, HEADS), 0)
    small = jnp.zeros((8, HEADS), F32)
    for n, part in enumerate(d3 + k3):
        small = jnp.where(r8 == n, part.astype(F32), small)
    small_wide = mm(small.astype(BF16), expand)
    b_t = mm_nt(eye, b_ref[...]).astype(BF16)
    state_t = mm(b_t, xw)
    small_bf = jnp.concatenate([small_wide, small_wide], axis=0).astype(BF16)
    for l in range(NP):
        lanes = slice(l * 128, (l + 1) * 128)
        msg1[l, 0:128, :] = state_t[:, lanes].astype(BF16)
        msg1[l, 128:144, :] = small_bf[:, lanes]

    pl.semaphore_wait(barrier, NP - 1 + NZ - 1 + 2)

    def exchange(sent, landed, send_sem, recv_sem, across):
        mine = plane if across else spot

        def one(i, carry):
            q = shifted(me, i * NP if across else i, 1)
            pltpu.make_async_remote_copy(
                src_ref=sent.at[q // NP if across else lax.rem(q, NP)], dst_ref=landed.at[mine],
                send_sem=send_sem, recv_sem=recv_sem, device_id=(q, y), device_id_type=MESH,
            ).start()
            return carry

        lax.fori_loop(1, NP, one, 0)
        landed[pl.ds(mine, 1)] = sent[pl.ds(mine, 1)]

    def exchanged(landed, send_sem, recv_sem):
        part = landed.at[pl.ds(0, NP - 1)]
        return pltpu.make_async_remote_copy(
            src_ref=part, dst_ref=part, send_sem=send_sem, recv_sem=recv_sem,
            device_id=(me, up_y), device_id_type=MESH,
        )

    exchange(msg1, recv1, xsem_s.at[0], xsem_r.at[0], False)

    e_hi, e_lo = split2(jnp.exp(cum))
    expcum[...] = mm(e_hi, expand) + mm(e_lo, expand)
    scores = mm_nt(c_ref[...], b_ref[...]) * causal
    low_half = (iota((TOK, 128), 1) < 64).astype(F32)
    skip_wide = small_wide[3:4, :] + small_wide[4:5, :] + small_wide[5:6, :]
    for l in range(8):
        lanes = slice(l * 128, (l + 1) * 128)
        mixes = []
        for h in (2 * l, 2 * l + 1):
            gap = jnp.minimum(cum[:, h : h + 1] - cum_t[h : h + 1, :], 0.0)
            mixes.append((jnp.exp(gap) * scores * dt_t[h : h + 1, :]).astype(BF16))
        x_l = x_wide[:, lanes]
        x_lo = x_l * low_half
        rhs = jnp.concatenate([x_lo.astype(BF16), (x_l - x_lo).astype(BF16)], axis=0)
        ybuf[:, lanes] = mm(jnp.concatenate(mixes, axis=1), rhs) + skip_wide[:, lanes] * x_l
        z_l = z_ref[:, lanes].astype(F32)
        szbuf[:, lanes] = 0.5 * z_l * (1.0 + jnp.tanh(0.5 * z_l))

    routes_t = routes_ref[...]
    rw_t = rw_ref[...]
    zme, xme, cme = me // 8, lax.rem(me // 2, 4), lax.rem(me, 2)
    dz = ((routes_t >> 3) - zme + 8) & 7
    group = jnp.zeros_like(dz)
    for n, value in enumerate(DZ):
        group = jnp.where(dz == value, n, group)
    off = group * 8 + ((((routes_t >> 1) & 3) - xme + 4) & 3) * 2 + (((routes_t & 1) - cme + 2) & 1)
    place = iota((NS, TOK), 0)
    first = off[0:1, :] == place
    second = off[1:2, :] == place
    named = jnp.where(first, 1.0, 0.0) + jnp.where(second, 1.0, 0.0)
    weight = jnp.where(first, rw_t[0:1, :], 0.0) + jnp.where(second, rw_t[1:2, :], 0.0)
    before = (rows < cols).astype(BF16)
    rank = mm(named.astype(BF16), before)
    rank = jnp.where(named > 0.5, rank, -1.0)
    slot_id = iota((NS, SLOTS, TOK), 1).astype(F32)
    hit = jnp.broadcast_to(rank[:, None, :], (NS, SLOTS, TOK)) == slot_id
    pick = jnp.where(hit, 1.0, 0.0).reshape(NS * SLOTS, TOK).astype(BF16)
    pick_w = jnp.where(hit, jnp.broadcast_to(weight[:, None, :], (NS, SLOTS, TOK)), 0.0).reshape(NS * SLOTS, TOK)
    pw_hi, pw_lo = split2(pick_w)
    wts[0] = mm_nt(eye, pw_hi).astype(BF16)
    wts[1] = mm_nt(eye, pw_lo).astype(BF16)

    loads[0].wait()
    sel16 = (iota((16, 128), 1) == iota((16, 128), 0) + plane * 16).astype(F32)
    state = mm_nt(sel16, init_v[...], HI)
    exchanged(recv1, xsem_s.at[0], xsem_r.at[0]).wait_recv()
    total = jnp.zeros((128, 128), F32)
    decay = jnp.ones((1, 128), F32)
    for j in range(NP):
        inner[j] = total
        through[j : j + 1, :] = decay
        step = recv1[j, 128:144, :].astype(F32)
        step = step[0:1, :] + step[1:2, :] + step[2:3, :]
        total = step * total + recv1[j, 0:128, :].astype(F32)
        decay = step * decay
    r16 = iota((16, 128), 0)
    tail = jnp.zeros((16, 128), F32)
    for n, part in enumerate(split3(decay)):
        tail = jnp.where(r16 == n, part.astype(F32), tail)
    for j in range(NZ):
        msg2[j, 0:16, :] = total[j * 16 : (j + 1) * 16, :].astype(BF16)
        msg2[j, 16:32, :] = tail.astype(BF16)
    exchange(msg2, recv2, xsem_s.at[1], xsem_r.at[1], True)
    exchanged(recv2, xsem_s.at[1], xsem_r.at[1]).wait_recv()
    for j in range(NZ):
        msg3[j] = state.astype(BF16)
        piece = recv2[j].astype(F32)
        state = (piece[16:17, :] + piece[17:18, :] + piece[18:19, :]) * state + piece[0:16, :]
    exchange(msg3, recv3, xsem_s.at[2], xsem_r.at[2], True)
    exchanged(recv3, xsem_s.at[2], xsem_r.at[2]).wait_recv()
    entry = recv3[...].astype(F32).reshape(128, 128)
    for j in range(NP):
        msg4[j] = (through[j : j + 1, :] * entry + inner[j]).astype(BF16)
    exchange(msg4, recv4, xsem_s.at[3], xsem_r.at[3], False)
    exchanged(recv4, xsem_s.at[3], xsem_r.at[3]).wait_recv()

    same_head = (iota((128, 128), 0) // 64 == iota((128, 128), 1) // 64).astype(BF16)
    c_bf = c_ref[...]
    for l in range(8):
        lanes = slice(l * 128, (l + 1) * 128)
        v = ybuf[:, lanes] + mm(c_bf, recv4[l]) * expcum[:, lanes]
        v = v * szbuf[:, lanes]
        mean_sq = mm((v * v).astype(BF16), same_head) * (1.0 / 64.0)
        normed[:, lanes] = (v * lax.rsqrt(mean_sq + 1e-05) * ngain_ref[:, lanes]).astype(BF16)

    def rs_copy(n, k):
        sent, landed, side = (far_s, far_r, k) if k < 2 else (near_s, near_r, k - 2)
        return pltpu.make_async_remote_copy(
            src_ref=sent.at[n, side], dst_ref=landed.at[n, side],
            send_sem=rs_s.at[n, k], recv_sem=rs_r.at[n, k],
            device_id=(me, dn_y if side else up_y), device_id_type=MESH,
        )

    half = TOK // 2

    def rs_begin(n, lhs, w_v):
        part = mm(lhs, w_v[:, pl.ds(pl.multiple_of(far_y * SLICE, SLICE), SLICE)]).astype(BF16)
        far_s[n, 0] = part[:half]
        far_s[n, 1] = part[half:]
        rs_copy(n, 0).start()
        rs_copy(n, 1).start()
        for slot, where in ((0, up_y), (1, dn_y), (2, y)):
            pbuf[n, slot] = mm(lhs, w_v[:, pl.ds(pl.multiple_of(where * SLICE, SLICE), SLICE)])

    def rs_middle(n):
        rs_copy(n, 0).wait_recv()
        near_s[n, 0, :half] = (pbuf[n, 0, :half] + far_r[n, 0].astype(F32)).astype(BF16)
        near_s[n, 0, half:] = pbuf[n, 0, half:].astype(BF16)
        rs_copy(n, 2).start()
        rs_copy(n, 1).wait_recv()
        near_s[n, 1, :half] = pbuf[n, 1, :half].astype(BF16)
        near_s[n, 1, half:] = (pbuf[n, 1, half:] + far_r[n, 1].astype(F32)).astype(BF16)
        rs_copy(n, 3).start()

    def rs_end(n):
        rs_copy(n, 2).wait_recv()
        rs_copy(n, 3).wait_recv()
        return pbuf[n, 2] + near_r[n, 0].astype(F32) + near_r[n, 1].astype(F32)

    loads[2].wait()
    rs_begin(GROUPS, normed[...], wout_v)
    loads[1].wait()
    rs_middle(GROUPS)
    hidden = (tok_v[...].astype(F32) + rs_end(GROUPS)).astype(BF16)
    hid[...] = hidden
    disp[...] = mm(pick, hidden).astype(BF16).reshape(NS, SLOTS, SLICE)

    def spread(k, sent, landed, send_sem, recv_sem, sign):
        def one(j, carry):
            i = k * NP + j
            pltpu.make_async_remote_copy(
                src_ref=sent.at[i], dst_ref=landed.at[i], send_sem=send_sem, recv_sem=recv_sem,
                device_id=(shifted(me, DZ[k] * NP + j, sign), y), device_id_type=MESH,
            ).start()
            return carry

        lax.fori_loop(0 if DZ[k] else 1, NP, one, 0)

    def gathered(k, landed, send_sem, recv_sem):
        first = 0 if DZ[k] else 1
        part = landed.at[pl.ds(k * NP + first, NP - first)]
        return pltpu.make_async_remote_copy(
            src_ref=part, dst_ref=part, send_sem=send_sem, recv_sem=recv_sem,
            device_id=(me, up_y), device_id_type=MESH,
        )

    own_x = xs.at[0]
    for k in range(NZ):
        spread(k, disp, own_x, sd, rd.at[k], 1)
    xs[0, OWN] = disp[OWN]
    for load in loads[3:]:
        load.wait()

    def ag_copy(g, k):
        src, dst, first, count, peer = (
            (0, 1, 0, NP, up_y),
            (0, 3, 0, NP, dn_y),
            (1, 2, 0, NP // 2, up_y),
            (3, 2, NP // 2, NP // 2, dn_y),
        )[k]
        part = pl.ds(g * NP + first, count)
        return pltpu.make_async_remote_copy(
            src_ref=xs.at[src, part], dst_ref=xs.at[dst, part],
            send_sem=ag_s.at[g, k], recv_sem=ag_r.at[g, k], device_id=(me, peer), device_id_type=MESH,
        )

    def arrive(k):
        gathered(k, own_x, sd, rd.at[k]).wait_recv()
        ag_copy(k, 0).start()
        ag_copy(k, 1).start()

    def forward(g):
        ag_copy(g, 0).wait_recv()
        ag_copy(g, 2).start()
        ag_copy(g, 1).wait_recv()
        ag_copy(g, 3).start()

    def expert(g):
        for k in (2 * g, 2 * g + 1):
            ag_copy(k, 2).wait_recv()
            ag_copy(k, 3).wait_recv()
        accg[...] = jnp.zeros_like(accg)
        accu[...] = jnp.zeros_like(accu)

        def piece(o, total):
            owner = lax.rem(y + NY - o, NY)
            at = pl.multiple_of(owner * SLICE, SLICE)
            v = xs[o, pl.ds(g * GS, GS)].astype(F32).reshape(TOK, SLICE)
            vg = (v * mgain_ref[:, pl.ds(at, SLICE)]).astype(BF16)
            accg[...] += mm(vg, wg_v[pl.ds(at, SLICE), :])
            accu[...] += mm(vg, wu_v[pl.ds(at, SLICE), :])
            return total + jnp.sum(v * v, axis=1, keepdims=True)

        total = lax.fori_loop(0, NY, piece, jnp.zeros((TOK, 1), F32))
        scale = lax.rsqrt(total * (1.0 / WIDTH) + 1e-05)
        gate = accg[...] * scale
        act = (0.5 * gate * (1.0 + jnp.tanh(0.5 * gate)) * (accu[...] * scale)).astype(BF16)
        rs_begin(g, act, wd_v)

    def give_back(g):
        rets[g * GS : (g + 1) * GS] = rs_end(g).astype(BF16).reshape(GS, SLOTS, SLICE)

        for k in (2 * g, 2 * g + 1):
            spread(k, rets, retr, sr, rr.at[k], -1)

    arrive(0)
    arrive(1)
    forward(0)
    arrive(2)
    forward(1)
    arrive(3)
    expert(0)
    forward(2)
    arrive(4)
    forward(3)
    arrive(5)
    expert(1)
    rs_middle(0)
    forward(4)
    arrive(6)
    forward(5)
    arrive(7)
    expert(2)
    rs_middle(1)
    give_back(0)
    forward(6)
    forward(7)
    expert(3)
    rs_middle(2)
    give_back(1)
    rs_middle(3)
    give_back(2)
    give_back(3)

    retr[OWN] = rets[OWN]
    total = hid[...].astype(F32)
    for g in range(GROUPS):
        for k in (2 * g, 2 * g + 1):
            gathered(k, retr, sr, rr.at[k]).wait_recv()
        back = retr[g * GS : (g + 1) * GS].reshape(TOK, SLICE)
        lanes = slice(g * TOK, (g + 1) * TOK)
        total = total + mm(wts[0, :, lanes], back) + mm(wts[1, :, lanes], back)
    out_ref[...] = total.astype(BF16)

    for n, buf in enumerate((msg1, msg2, msg3, msg4)):
        exchanged(buf, xsem_s.at[n], xsem_r.at[n]).wait_send()
    for buf, sem in ((disp, sd), (rets, sr)):
        part = buf.at[pl.ds(0, NS - 1)]
        pltpu.make_async_remote_copy(
            src_ref=part, dst_ref=part, send_sem=sem, recv_sem=rd.at[0],
            device_id=(me, up_y), device_id_type=MESH,
        ).wait_send()
    for g in range(NZ):
        for k in range(4):
            ag_copy(g, k).wait_send()
    for n in range(GROUPS + 1):
        for k in range(4):
            rs_copy(n, k).wait_send()


def body(
    tokens, input_heads, z_gate, b_proj, c_proj, step_size, decay_log, skip_gain, init_state, norm_gain,
    out_weight, moe_gain, routes, route_weights, w_gate, w_up, w_down,
):
    vmem = pl.BlockSpec(memory_space=pltpu.VMEM)
    hbm = pl.BlockSpec(memory_space=pl.ANY)
    dma = pltpu.SemaphoreType.DMA
    n = GROUPS + 1
    scratch = [
        pltpu.VMEM((NP, 144, 128), BF16),
        pltpu.VMEM((NP, 144, 128), BF16),
        pltpu.VMEM((NZ, 32, 128), BF16),
        pltpu.VMEM((NZ, 32, 128), BF16),
        pltpu.VMEM((NZ, 16, 128), BF16),
        pltpu.VMEM((NZ, 16, 128), BF16),
        pltpu.VMEM((NP, 128, 128), BF16),
        pltpu.VMEM((NP, 128, 128), BF16),
        pltpu.VMEM((NP, 128, 128), F32),
        pltpu.VMEM((NP, 128), F32),
        pltpu.VMEM((TOK, INNER), F32),
        pltpu.VMEM((TOK, INNER), F32),
        pltpu.VMEM((TOK, INNER), F32),
        pltpu.VMEM((TOK, INNER), BF16),
        pltpu.VMEM((TOK, SLICE), BF16),
        pltpu.VMEM((128, 128), F32),
        pltpu.VMEM((INNER, WIDTH), BF16),
        pltpu.VMEM((WIDTH, SLICE), BF16),
        pltpu.VMEM((WIDTH, SLICE), BF16),
        pltpu.VMEM((SLICE, WIDTH), BF16),
        pltpu.VMEM((NS, SLOTS, SLICE), BF16),
        pltpu.VMEM((NY, NS, SLOTS, SLICE), BF16),
        pltpu.VMEM((TOK, SLICE), F32),
        pltpu.VMEM((TOK, SLICE), F32),
        pltpu.VMEM((TOK, SLICE), BF16),
        pltpu.VMEM((2, TOK, NS * SLOTS), BF16),
        pltpu.VMEM((n, 2, TOK // 2, SLICE), BF16),
        pltpu.VMEM((n, 2, TOK // 2, SLICE), BF16),
        pltpu.VMEM((n, 2, TOK, SLICE), BF16),
        pltpu.VMEM((n, 2, TOK, SLICE), BF16),
        pltpu.VMEM((n, 3, TOK, SLICE), F32),
        pltpu.VMEM((NS, SLOTS, SLICE), BF16),
        pltpu.VMEM((NS, SLOTS, SLICE), BF16),
        dma((6,)),
        dma((4,)), dma((4,)),
        dma, dma((NZ,)),
        dma, dma((NZ,)),
        dma((NZ, 4)), dma((NZ, 4)),
        dma((n, 4)), dma((n, 4)),
    ]
    return pl.pallas_call(
        kernel,
        out_shape=jax.ShapeDtypeStruct((TOK, SLICE), BF16),
        in_specs=[vmem] * 11 + [hbm] * 6,
        out_specs=vmem,
        scratch_shapes=scratch,
        name="mixer_moe",
        compiler_params=pltpu.CompilerParams(
            collective_id=0, has_side_effects=True, vmem_limit_bytes=56 * 1024 * 1024
        ),
    )(
        input_heads, z_gate, b_proj, c_proj, step_size.T, decay_log.T, skip_gain.reshape(1, HEADS),
        norm_gain.reshape(1, INNER), moe_gain.reshape(1, WIDTH), routes.T, route_weights.T,
        tokens, init_state.reshape(INNER, 128), out_weight, w_gate[0], w_up[0], w_down[0],
    )


def solution(mesh):
    in_specs = (
        P("seq", None),
        P("seq", "tp"),
        P("seq", "tp"),
        P("seq", None),
        P("seq", None),
        P("seq", "tp"),
        P("seq", "tp"),
        P("tp"),
        P("tp", None, None),
        P("tp"),
        P("tp", None),
        P(),
        P("seq", None),
        P("seq", None),
        P("seq", None, "tp"),
        P("seq", None, "tp"),
        P("seq", "tp", None),
    )
    return jax.shard_map(body, mesh=mesh, in_specs=in_specs, out_specs=P("seq", "tp"), check_vma=False)
```

```python
import functools

import jax
import jax.numpy as jnp
from jax import lax
from jax.experimental import pallas as pl
from jax.experimental.pallas import tpu as pltpu
from jax.sharding import PartitionSpec as P

F32 = jnp.float32
BF16 = jnp.bfloat16
HI = lax.Precision.HIGHEST
MESH = pl.DeviceIdType.MESH
NZ, NX, NC = 8, 4, 2
NS = NZ * NX * NC
NP = NX * NC
NY = 4
TOK = 128
HEADS = 16
INNER = 1024
WIDTH = 2048
SLICE = 512
SLOTS = 8
GROUPS = 8
GS = NS // GROUPS
GR = GS * SLOTS
PAIRS = GROUPS // 2
DZ = (0, 1, 7, 2, 6, 3, 5, 4)
OWN = DZ.index(0) * NP


def iota(shape, dim):
    return lax.broadcasted_iota(jnp.int32, shape, dim)


def mm(a, b):
    return jnp.dot(a, b, preferred_element_type=F32)


def mm_nt(a, b, precision=None):
    return lax.dot_general(a, b, (((1,), (1,)), ((), ())), precision=precision, preferred_element_type=F32)


def split2(v):
    hi = v.astype(BF16)
    return hi, (v - hi.astype(F32)).astype(BF16)


def split3(v):
    hi, mid = split2(v)
    low = (v - hi.astype(F32) - mid.astype(F32)).astype(BF16)
    return hi, mid, low


def kernel(
    x_ref, z_ref, b_ref, c_ref, dt_ref, la_ref, skip_ref, ngain_ref, mgain_ref, routes_ref, rw_ref,
    tokens_hbm, init_hbm, wout_hbm, wg_hbm, wu_hbm, wd_hbm,
    out_ref,
    msg1, recv1, msg2, recv2, msg3, recv3, msg4, recv4, inner, through, ybuf, szbuf, expcum, normed,
    tok_v, init_v, wout_v, wg_v, wu_v, wd_v,
    disp, xs, accg, accu, hid, wts,
    far_s, far_r, near_s, near_r, pbuf, rets, retr,
    wsem, xsem_s, xsem_r, sd, rd, sr, rr, ag_s, ag_r, rs_s, rs_r,
):
    me = lax.axis_index("seq")
    y = lax.axis_index("tp")
    up_y = lax.rem(y + 1, NY)
    dn_y = lax.rem(y + NY - 1, NY)
    far_y = lax.rem(y + 2, NY)

    zme, xme, cme = me // NP, lax.rem(me, NP) // NC, lax.rem(me, NC)
    planes = [lax.rem(zme + n, NZ) for n in range(NZ)]
    z_terms = [z * NP for z in planes]
    x_terms = [lax.rem(xme + n, NX) * NC for n in range(NX)]
    c_terms = [cme, 1 - cme]
    spots = [x_terms[n // NC] + c_terms[n % NC] for n in range(NP)]
    spots_back = [x_terms[-(n // NC) % NX] + c_terms[n % NC] for n in range(NP)]

    barrier = pltpu.get_barrier_semaphore()
    plane, spot = zme, spots[0]
    for peer in [z_terms[0] + s for s in spots[1:]] + [z + spot for z in z_terms[1:]]:
        pl.semaphore_signal(barrier, inc=1, device_id=(peer, y), device_id_type=MESH)
    for peer in (up_y, dn_y):
        pl.semaphore_signal(barrier, inc=1, device_id=(me, peer), device_id_type=MESH)

    own_col = pl.multiple_of(y * SLICE, SLICE)
    tile_row = pl.multiple_of(spot * 128, 128)
    loads = [
        pltpu.make_async_copy(init_hbm.at[pl.ds(tile_row, 128), :], init_v, wsem.at[0]),
        pltpu.make_async_copy(tokens_hbm.at[:, pl.ds(own_col, SLICE)], tok_v, wsem.at[1]),
        pltpu.make_async_copy(wout_hbm, wout_v, wsem.at[2]),
        pltpu.make_async_copy(wg_hbm, wg_v, wsem.at[3]),
        pltpu.make_async_copy(wu_hbm, wu_v, wsem.at[4]),
        pltpu.make_async_copy(wd_hbm, wd_v, wsem.at[5]),
    ]
    for load in loads:
        load.start()

    rows = iota((TOK, TOK), 0)
    cols = iota((TOK, TOK), 1)
    causal = (rows >= cols).astype(F32)
    eye = (rows == cols).astype(BF16)
    eye_f = eye.astype(F32)
    dt_t = dt_ref[...]
    cum_t = mm_nt(la_ref[...], causal, HI)
    cum = mm_nt(eye_f, cum_t, HI)
    dt = mm_nt(eye_f, dt_t, HI)
    end = cum[TOK - 1 : TOK, :]
    expand = (iota((HEADS, INNER), 1) // 64 == iota((HEADS, INNER), 0)).astype(BF16)
    w_hi, w_lo = split2(jnp.exp(end - cum) * dt)
    w_wide = mm(w_hi, expand) + mm(w_lo, expand)
    x_wide = x_ref[...].astype(F32)
    xw = (x_wide * w_wide).astype(BF16)
    d3 = split3(jnp.exp(end))
    k3 = split3(skip_ref[...])
    r8 = iota((8, HEADS), 0)
    small = jnp.zeros((8, HEADS), F32)
    for n, part in enumerate(d3 + k3):
        small = jnp.where(r8 == n, part.astype(F32), small)
    small_wide = mm(small.astype(BF16), expand)
    b_t = mm_nt(eye, b_ref[...]).astype(BF16)
    state_t = mm(b_t, xw)
    small_bf = jnp.concatenate([small_wide, small_wide], axis=0).astype(BF16)
    for l in range(NP):
        lanes = slice(l * 128, (l + 1) * 128)
        msg1[l, 0:128, :] = state_t[:, lanes].astype(BF16)
        msg1[l, 128:144, :] = small_bf[:, lanes]

    pl.semaphore_wait(barrier, NP - 1 + NZ - 1 + 2)

    def exchange(sent, landed, send_sem, recv_sem, across):
        mine = plane if across else spot
        for n in range(1, NP):
            other = planes[n] if across else spots[n]
            peer = z_terms[n] + spot if across else z_terms[0] + spots[n]
            pltpu.make_async_remote_copy(
                src_ref=sent.at[other], dst_ref=landed.at[mine],
                send_sem=send_sem, recv_sem=recv_sem, device_id=(peer, y), device_id_type=MESH,
            ).start()
        landed[pl.ds(mine, 1)] = sent[pl.ds(mine, 1)]

    def exchanged(landed, send_sem, recv_sem):
        part = landed.at[pl.ds(0, NP - 1)]
        return pltpu.make_async_remote_copy(
            src_ref=part, dst_ref=part, send_sem=send_sem, recv_sem=recv_sem,
            device_id=(me, up_y), device_id_type=MESH,
        )

    exchange(msg1, recv1, xsem_s.at[0], xsem_r.at[0], False)

    e_hi, e_lo = split2(jnp.exp(cum))
    expcum[...] = mm(e_hi, expand) + mm(e_lo, expand)
    scores = mm_nt(c_ref[...], b_ref[...]) * causal
    low_half = (iota((TOK, 128), 1) < 64).astype(F32)
    skip_wide = small_wide[3:4, :] + small_wide[4:5, :] + small_wide[5:6, :]
    for l in range(8):
        lanes = slice(l * 128, (l + 1) * 128)
        mixes = []
        for h in (2 * l, 2 * l + 1):
            gap = jnp.minimum(cum[:, h : h + 1] - cum_t[h : h + 1, :], 0.0)
            mixes.append((jnp.exp(gap) * scores * dt_t[h : h + 1, :]).astype(BF16))
        x_l = x_wide[:, lanes]
        x_lo = x_l * low_half
        rhs = jnp.concatenate([x_lo.astype(BF16), (x_l - x_lo).astype(BF16)], axis=0)
        ybuf[:, lanes] = mm(jnp.concatenate(mixes, axis=1), rhs) + skip_wide[:, lanes] * x_l
        z_l = z_ref[:, lanes].astype(F32)
        szbuf[:, lanes] = 0.5 * z_l * (1.0 + jnp.tanh(0.5 * z_l))

    routes_t = routes_ref[...]
    rw_t = rw_ref[...]
    dz = ((routes_t >> 3) - zme + 8) & 7
    group = jnp.zeros_like(dz)
    for n, value in enumerate(DZ):
        group = jnp.where(dz == value, n, group)
    off = group * 8 + ((((routes_t >> 1) & 3) - xme + 4) & 3) * 2 + (((routes_t & 1) - cme + 2) & 1)
    place = iota((NS, TOK), 0)
    first = off[0:1, :] == place
    second = off[1:2, :] == place
    named = jnp.where(first, 1.0, 0.0) + jnp.where(second, 1.0, 0.0)
    weight = jnp.where(first, rw_t[0:1, :], 0.0) + jnp.where(second, rw_t[1:2, :], 0.0)
    before = (rows < cols).astype(BF16)
    rank = mm(named.astype(BF16), before)
    rank = jnp.where(named > 0.5, rank, -1.0)
    slot_id = iota((NS, SLOTS, TOK), 1).astype(F32)
    hit = jnp.broadcast_to(rank[:, None, :], (NS, SLOTS, TOK)) == slot_id
    pick = jnp.where(hit, 1.0, 0.0).reshape(NS * SLOTS, TOK).astype(BF16)
    pick_w = jnp.where(hit, jnp.broadcast_to(weight[:, None, :], (NS, SLOTS, TOK)), 0.0).reshape(NS * SLOTS, TOK)
    pw_hi, pw_lo = split2(pick_w)
    wts[0] = mm_nt(eye, pw_hi).astype(BF16)
    wts[1] = mm_nt(eye, pw_lo).astype(BF16)

    loads[0].wait()
    sel16 = (iota((16, 128), 1) == iota((16, 128), 0) + plane * 16).astype(F32)
    state = mm_nt(sel16, init_v[...], HI)
    exchanged(recv1, xsem_s.at[0], xsem_r.at[0]).wait_recv()
    total = jnp.zeros((128, 128), F32)
    decay = jnp.ones((1, 128), F32)
    for j in range(NP):
        inner[j] = total
        through[j : j + 1, :] = decay
        step = recv1[j, 128:144, :].astype(F32)
        step = step[0:1, :] + step[1:2, :] + step[2:3, :]
        total = step * total + recv1[j, 0:128, :].astype(F32)
        decay = step * decay
    r16 = iota((16, 128), 0)
    tail = jnp.zeros((16, 128), F32)
    for n, part in enumerate(split3(decay)):
        tail = jnp.where(r16 == n, part.astype(F32), tail)
    for j in range(NZ):
        msg2[j, 0:16, :] = total[j * 16 : (j + 1) * 16, :].astype(BF16)
        msg2[j, 16:32, :] = tail.astype(BF16)
    exchange(msg2, recv2, xsem_s.at[1], xsem_r.at[1], True)
    exchanged(recv2, xsem_s.at[1], xsem_r.at[1]).wait_recv()
    for j in range(NZ):
        msg3[j] = state.astype(BF16)
        piece = recv2[j].astype(F32)
        state = (piece[16:17, :] + piece[17:18, :] + piece[18:19, :]) * state + piece[0:16, :]
    exchange(msg3, recv3, xsem_s.at[2], xsem_r.at[2], True)
    exchanged(recv3, xsem_s.at[2], xsem_r.at[2]).wait_recv()
    entry = recv3[...].astype(F32).reshape(128, 128)
    for j in range(NP):
        msg4[j] = (through[j : j + 1, :] * entry + inner[j]).astype(BF16)
    exchange(msg4, recv4, xsem_s.at[3], xsem_r.at[3], False)
    exchanged(recv4, xsem_s.at[3], xsem_r.at[3]).wait_recv()

    same_head = (iota((128, 128), 0) // 64 == iota((128, 128), 1) // 64).astype(BF16)
    c_bf = c_ref[...]
    for l in range(8):
        lanes = slice(l * 128, (l + 1) * 128)
        v = ybuf[:, lanes] + mm(c_bf, recv4[l]) * expcum[:, lanes]
        v = v * szbuf[:, lanes]
        mean_sq = mm((v * v).astype(BF16), same_head) * (1.0 / 64.0)
        normed[:, lanes] = (v * lax.rsqrt(mean_sq + 1e-05) * ngain_ref[:, lanes]).astype(BF16)

    def rs_copy(n, k):
        sent, landed, side = (far_s, far_r, k) if k < 2 else (near_s, near_r, k - 2)
        return pltpu.make_async_remote_copy(
            src_ref=sent.at[n, side], dst_ref=landed.at[n, side],
            send_sem=rs_s.at[n, k], recv_sem=rs_r.at[n, k],
            device_id=(me, dn_y if side else up_y), device_id_type=MESH,
        )

    half = GR // 2

    def columns(w_v, where):
        return w_v[:, pl.ds(pl.multiple_of(where * SLICE, SLICE), SLICE)]

    def rs_begin(pair, lhs, w_v):
        part = mm(lhs, columns(w_v, far_y)).astype(BF16)
        for n in (0, 1):
            far_s[2 * pair + n, 0] = part[n * GR : n * GR + half]
            far_s[2 * pair + n, 1] = part[n * GR + half : (n + 1) * GR]
            rs_copy(2 * pair + n, 0).start()
            rs_copy(2 * pair + n, 1).start()
        for slot, where in ((0, up_y), (1, dn_y), (2, y)):
            part = mm(lhs, columns(w_v, where))
            pbuf[2 * pair, slot] = part[:GR]
            pbuf[2 * pair + 1, slot] = part[GR:]

    def rs_middle(n):
        rs_copy(n, 0).wait_recv()
        near_s[n, 0, :half] = (pbuf[n, 0, :half] + far_r[n, 0].astype(F32)).astype(BF16)
        near_s[n, 0, half:] = pbuf[n, 0, half:].astype(BF16)
        rs_copy(n, 2).start()
        rs_copy(n, 1).wait_recv()
        near_s[n, 1, :half] = pbuf[n, 1, :half].astype(BF16)
        near_s[n, 1, half:] = (pbuf[n, 1, half:] + far_r[n, 1].astype(F32)).astype(BF16)
        rs_copy(n, 3).start()

    def rs_end(n):
        rs_copy(n, 2).wait_recv()
        rs_copy(n, 3).wait_recv()
        return pbuf[n, 2] + near_r[n, 0].astype(F32) + near_r[n, 1].astype(F32)

    loads[2].wait()
    rs_begin(PAIRS, normed[...], wout_v)
    loads[1].wait()
    rs_middle(GROUPS)
    rs_middle(GROUPS + 1)
    summed = jnp.concatenate([rs_end(GROUPS), rs_end(GROUPS + 1)], axis=0)
    hidden = (tok_v[...].astype(F32) + summed).astype(BF16)
    hid[...] = hidden
    disp[...] = mm(pick, hidden).astype(BF16).reshape(NS, SLOTS, SLICE)

    def spread(k, sent, landed, send_sem, recv_sem, sign):
        for j in range(0 if DZ[k] else 1, NP):
            i = k * NP + j
            dest = z_terms[sign * DZ[k] % NZ] + (spots if sign > 0 else spots_back)[j]
            pltpu.make_async_remote_copy(
                src_ref=sent.at[i], dst_ref=landed.at[i], send_sem=send_sem, recv_sem=recv_sem,
                device_id=(dest, y), device_id_type=MESH,
            ).start()

    def gathered(k, landed, send_sem, recv_sem):
        first = 0 if DZ[k] else 1
        part = landed.at[pl.ds(k * NP + first, NP - first)]
        return pltpu.make_async_remote_copy(
            src_ref=part, dst_ref=part, send_sem=send_sem, recv_sem=recv_sem,
            device_id=(me, up_y), device_id_type=MESH,
        )

    own_x = xs.at[0]
    for k in range(NZ):
        spread(k, disp, own_x, sd, rd.at[k], 1)
    xs[0, OWN] = disp[OWN]
    for load in loads[3:]:
        load.wait()

    def ag_copy(g, k):
        src, dst, first, count, peer = (
            (0, 1, 0, NP, up_y),
            (0, 3, 0, NP, dn_y),
            (1, 2, 0, NP // 2, up_y),
            (3, 2, NP // 2, NP // 2, dn_y),
        )[k]
        part = pl.ds(g * NP + first, count)
        return pltpu.make_async_remote_copy(
            src_ref=xs.at[src, part], dst_ref=xs.at[dst, part],
            send_sem=ag_s.at[g, k], recv_sem=ag_r.at[g, k], device_id=(me, peer), device_id_type=MESH,
        )

    def arrive(k):
        gathered(k, own_x, sd, rd.at[k]).wait_recv()
        ag_copy(k, 0).start()
        ag_copy(k, 1).start()

    def forward(g):
        ag_copy(g, 0).wait_recv()
        ag_copy(g, 2).start()
        ag_copy(g, 1).wait_recv()
        ag_copy(g, 3).start()

    def expert(pair):
        for g in (2 * pair, 2 * pair + 1):
            ag_copy(g, 2).wait_recv()
            ag_copy(g, 3).wait_recv()
        accg[...] = jnp.zeros_like(accg)
        accu[...] = jnp.zeros_like(accu)

        def piece(o, total):
            owner = lax.rem(y + NY - o, NY)
            at = pl.multiple_of(owner * SLICE, SLICE)
            v = xs[o, pl.ds(2 * pair * GS, 2 * GS)].astype(F32).reshape(2 * GR, SLICE)
            vg = (v * mgain_ref[:, pl.ds(at, SLICE)]).astype(BF16)
            accg[...] += mm(vg, wg_v[pl.ds(at, SLICE), :])
            accu[...] += mm(vg, wu_v[pl.ds(at, SLICE), :])
            return total + jnp.sum(v * v, axis=1, keepdims=True)

        total = lax.fori_loop(0, NY, piece, jnp.zeros((2 * GR, 1), F32))
        scale = lax.rsqrt(total * (1.0 / WIDTH) + 1e-05)
        gate = accg[...] * scale
        act = (0.5 * gate * (1.0 + jnp.tanh(0.5 * gate)) * (accu[...] * scale)).astype(BF16)
        rs_begin(pair, act, wd_v)

    def give_back(g):
        rets[g * GS : (g + 1) * GS] = rs_end(g).astype(BF16).reshape(GS, SLOTS, SLICE)

        spread(g, rets, retr, sr, rr.at[g], -1)

    arrive(0)
    arrive(1)
    forward(0)
    arrive(2)
    forward(1)
    arrive(3)
    forward(2)
    arrive(4)
    forward(3)
    arrive(5)
    forward(4)
    expert(0)
    arrive(6)
    forward(5)
    arrive(7)
    forward(6)
    expert(1)
    rs_middle(0)
    rs_middle(1)
    forward(7)
    expert(2)
    rs_middle(2)
    rs_middle(3)
    give_back(0)
    give_back(1)
    expert(3)
    rs_middle(4)
    rs_middle(5)
    give_back(2)
    give_back(3)
    rs_middle(6)
    rs_middle(7)
    give_back(4)
    give_back(5)
    give_back(6)
    give_back(7)

    retr[OWN] = rets[OWN]
    total = hid[...].astype(F32)
    for g in range(GROUPS):
        gathered(g, retr, sr, rr.at[g]).wait_recv()
        if g % 2:
            back = retr[(g - 1) * GS : (g + 1) * GS].reshape(2 * GR, SLICE)
            lanes = slice((g - 1) * GR, (g + 1) * GR)
            total = total + mm(wts[0, :, lanes], back) + mm(wts[1, :, lanes], back)
    out_ref[...] = total.astype(BF16)

    for n, buf in enumerate((msg1, msg2, msg3, msg4)):
        exchanged(buf, xsem_s.at[n], xsem_r.at[n]).wait_send()
    for buf, sem in ((disp, sd), (rets, sr)):
        part = buf.at[pl.ds(0, NS - 1)]
        pltpu.make_async_remote_copy(
            src_ref=part, dst_ref=part, send_sem=sem, recv_sem=rd.at[0],
            device_id=(me, up_y), device_id_type=MESH,
        ).wait_send()
    for g in range(NZ):
        for k in range(4):
            ag_copy(g, k).wait_send()
    for n in range(GROUPS + 2):
        for k in range(4):
            rs_copy(n, k).wait_send()


def body(
    tokens, input_heads, z_gate, b_proj, c_proj, step_size, decay_log, skip_gain, init_state, norm_gain,
    out_weight, moe_gain, routes, route_weights, w_gate, w_up, w_down,
):
    vmem = pl.BlockSpec(memory_space=pltpu.VMEM)
    hbm = pl.BlockSpec(memory_space=pl.ANY)
    dma = pltpu.SemaphoreType.DMA
    n = GROUPS + 2
    scratch = [
        pltpu.VMEM((NP, 144, 128), BF16),
        pltpu.VMEM((NP, 144, 128), BF16),
        pltpu.VMEM((NZ, 32, 128), BF16),
        pltpu.VMEM((NZ, 32, 128), BF16),
        pltpu.VMEM((NZ, 16, 128), BF16),
        pltpu.VMEM((NZ, 16, 128), BF16),
        pltpu.VMEM((NP, 128, 128), BF16),
        pltpu.VMEM((NP, 128, 128), BF16),
        pltpu.VMEM((NP, 128, 128), F32),
        pltpu.VMEM((NP, 128), F32),
        pltpu.VMEM((TOK, INNER), F32),
        pltpu.VMEM((TOK, INNER), F32),
        pltpu.VMEM((TOK, INNER), F32),
        pltpu.VMEM((TOK, INNER), BF16),
        pltpu.VMEM((TOK, SLICE), BF16),
        pltpu.VMEM((128, 128), F32),
        pltpu.VMEM((INNER, WIDTH), BF16),
        pltpu.VMEM((WIDTH, SLICE), BF16),
        pltpu.VMEM((WIDTH, SLICE), BF16),
        pltpu.VMEM((SLICE, WIDTH), BF16),
        pltpu.VMEM((NS, SLOTS, SLICE), BF16),
        pltpu.VMEM((NY, NS, SLOTS, SLICE), BF16),
        pltpu.VMEM((2 * GR, SLICE), F32),
        pltpu.VMEM((2 * GR, SLICE), F32),
        pltpu.VMEM((TOK, SLICE), BF16),
        pltpu.VMEM((2, TOK, NS * SLOTS), BF16),
        pltpu.VMEM((n, 2, GR // 2, SLICE), BF16),
        pltpu.VMEM((n, 2, GR // 2, SLICE), BF16),
        pltpu.VMEM((n, 2, GR, SLICE), BF16),
        pltpu.VMEM((n, 2, GR, SLICE), BF16),
        pltpu.VMEM((n, 3, GR, SLICE), F32),
        pltpu.VMEM((NS, SLOTS, SLICE), BF16),
        pltpu.VMEM((NS, SLOTS, SLICE), BF16),
        dma((6,)),
        dma((4,)), dma((4,)),
        dma, dma((NZ,)),
        dma, dma((NZ,)),
        dma((NZ, 4)), dma((NZ, 4)),
        dma((n, 4)), dma((n, 4)),
    ]
    return pl.pallas_call(
        kernel,
        out_shape=jax.ShapeDtypeStruct((TOK, SLICE), BF16),
        in_specs=[vmem] * 11 + [hbm] * 6,
        out_specs=vmem,
        scratch_shapes=scratch,
        name="mixer_moe",
        compiler_params=pltpu.CompilerParams(
            collective_id=0, has_side_effects=True, vmem_limit_bytes=56 * 1024 * 1024
        ),
    )(
        input_heads, z_gate, b_proj, c_proj, step_size.T, decay_log.T, skip_gain.reshape(1, HEADS),
        norm_gain.reshape(1, INNER), moe_gain.reshape(1, WIDTH), routes.T, route_weights.T,
        tokens, init_state.reshape(INNER, 128), out_weight, w_gate[0], w_up[0], w_down[0],
    )


def solution(mesh):
    in_specs = (
        P("seq", None),
        P("seq", "tp"),
        P("seq", "tp"),
        P("seq", None),
        P("seq", None),
        P("seq", "tp"),
        P("seq", "tp"),
        P("tp"),
        P("tp", None, None),
        P("tp"),
        P("tp", None),
        P(),
        P("seq", None),
        P("seq", None),
        P("seq", None, "tp"),
        P("seq", None, "tp"),
        P("seq", "tp", None),
    )
    return jax.shard_map(body, mesh=mesh, in_specs=in_specs, out_specs=P("seq", "tp"), check_vma=False)
```

```python
import functools

import jax
import jax.numpy as jnp
from jax import lax
from jax.experimental import pallas as pl
from jax.experimental.pallas import tpu as pltpu
from jax.sharding import PartitionSpec as P

F32 = jnp.float32
BF16 = jnp.bfloat16
HI = lax.Precision.HIGHEST
MESH = pl.DeviceIdType.MESH
NZ, NX, NC = 8, 4, 2
NS = NZ * NX * NC
NP = NX * NC
NY = 4
TOK = 128
HEADS = 16
INNER = 1024
WIDTH = 2048
SLICE = 512
SLOTS = 8
GROUPS = 8
GS = NS // GROUPS
GR = GS * SLOTS
PAIRS = GROUPS // 2
DZ = (0, 1, 7, 2, 6, 3, 5, 4)
OWN = DZ.index(0) * NP
FAR_Z = (4, 3, 5, 2, 6, 1, 7)
FAR_SPOT = (4, 5, 2, 3, 6, 7, 1, 0)


def iota(shape, dim):
    return lax.broadcasted_iota(jnp.int32, shape, dim)


def mm(a, b):
    return jnp.dot(a, b, preferred_element_type=F32)


def mm_nt(a, b, precision=None):
    return lax.dot_general(a, b, (((1,), (1,)), ((), ())), precision=precision, preferred_element_type=F32)


def split2(v):
    hi = v.astype(BF16)
    return hi, (v - hi.astype(F32)).astype(BF16)


def split3(v):
    hi, mid = split2(v)
    low = (v - hi.astype(F32) - mid.astype(F32)).astype(BF16)
    return hi, mid, low


def kernel(
    x_ref, z_ref, b_ref, c_ref, dt_ref, la_ref, skip_ref, ngain_ref, mgain_ref, routes_ref, rw_ref,
    tokens_hbm, init_hbm, wout_hbm, wg_hbm, wu_hbm, wd_hbm,
    out_ref,
    msg1, recv1, msg2, recv2, msg3, recv3, msg4, recv4, inner, through, ybuf, szbuf, expcum, normed,
    tok_v, init_v, wout_v, wg_v, wu_v, wd_v,
    disp, xs, accg, accu, hid, wts,
    far_s, far_r, near_s, near_r, pbuf, rets, retr,
    wsem, xsem_s, xsem_r, sd, rd, sr, rr, ag_s, ag_r, rs_s, rs_r,
):
    me = lax.axis_index("seq")
    y = lax.axis_index("tp")
    up_y = lax.rem(y + 1, NY)
    dn_y = lax.rem(y + NY - 1, NY)
    far_y = lax.rem(y + 2, NY)

    zme, xme, cme = me // NP, lax.rem(me, NP) // NC, lax.rem(me, NC)
    planes = [lax.rem(zme + n, NZ) for n in range(NZ)]
    z_terms = [z * NP for z in planes]
    x_terms = [lax.rem(xme + n, NX) * NC for n in range(NX)]
    c_terms = [cme, 1 - cme]
    spots = [x_terms[n // NC] + c_terms[n % NC] for n in range(NP)]
    spots_back = [x_terms[-(n // NC) % NX] + c_terms[n % NC] for n in range(NP)]

    barrier = pltpu.get_barrier_semaphore()
    plane, spot = zme, spots[0]
    for peer in [z_terms[n] + spot for n in FAR_Z] + [z_terms[0] + spots[n] for n in FAR_SPOT if n]:
        pl.semaphore_signal(barrier, inc=1, device_id=(peer, y), device_id_type=MESH)
    for peer in (up_y, dn_y):
        pl.semaphore_signal(barrier, inc=1, device_id=(me, peer), device_id_type=MESH)

    own_col = pl.multiple_of(y * SLICE, SLICE)
    tile_row = pl.multiple_of(spot * 128, 128)
    loads = [
        pltpu.make_async_copy(init_hbm.at[pl.ds(tile_row, 128), :], init_v, wsem.at[0]),
        pltpu.make_async_copy(tokens_hbm.at[:, pl.ds(own_col, SLICE)], tok_v, wsem.at[1]),
        pltpu.make_async_copy(wout_hbm, wout_v, wsem.at[2]),
        pltpu.make_async_copy(wg_hbm, wg_v, wsem.at[3]),
        pltpu.make_async_copy(wu_hbm, wu_v, wsem.at[4]),
        pltpu.make_async_copy(wd_hbm, wd_v, wsem.at[5]),
    ]
    for load in loads:
        load.start()

    rows = iota((TOK, TOK), 0)
    cols = iota((TOK, TOK), 1)
    causal = (rows >= cols).astype(F32)
    eye = (rows == cols).astype(BF16)
    eye_f = eye.astype(F32)
    dt_t = dt_ref[...]
    cum_t = mm_nt(la_ref[...], causal, HI)
    cum = mm_nt(eye_f, cum_t, HI)
    dt = mm_nt(eye_f, dt_t, HI)
    end = cum[TOK - 1 : TOK, :]
    expand = (iota((HEADS, INNER), 1) // 64 == iota((HEADS, INNER), 0)).astype(BF16)
    w_hi, w_lo = split2(jnp.exp(end - cum) * dt)
    w_wide = mm(w_hi, expand) + mm(w_lo, expand)
    x_wide = x_ref[...].astype(F32)
    xw = (x_wide * w_wide).astype(BF16)
    d3 = split3(jnp.exp(end))
    k3 = split3(skip_ref[...])
    r8 = iota((8, HEADS), 0)
    small = jnp.zeros((8, HEADS), F32)
    for n, part in enumerate(d3 + k3):
        small = jnp.where(r8 == n, part.astype(F32), small)
    small_wide = mm(small.astype(BF16), expand)
    b_t = mm_nt(eye, b_ref[...]).astype(BF16)
    state_t = mm(b_t, xw)
    small_bf = jnp.concatenate([small_wide, small_wide], axis=0).astype(BF16)
    for l in range(NP):
        lanes = slice(l * 128, (l + 1) * 128)
        msg1[l, 0:128, :] = state_t[:, lanes].astype(BF16)
        msg1[l, 128:144, :] = small_bf[:, lanes]

    pl.semaphore_wait(barrier, NP - 1 + NZ - 1 + 2)

    def exchange(sent, landed, send_sem, recv_sem, across):
        mine = plane if across else spot
        for n in FAR_Z if across else FAR_SPOT:
            if n == 0:
                continue
            other = planes[n] if across else spots[n]
            peer = z_terms[n] + spot if across else z_terms[0] + spots[n]
            pltpu.make_async_remote_copy(
                src_ref=sent.at[other], dst_ref=landed.at[mine],
                send_sem=send_sem, recv_sem=recv_sem, device_id=(peer, y), device_id_type=MESH,
            ).start()
        landed[pl.ds(mine, 1)] = sent[pl.ds(mine, 1)]

    def exchanged(landed, send_sem, recv_sem):
        part = landed.at[pl.ds(0, NP - 1)]
        return pltpu.make_async_remote_copy(
            src_ref=part, dst_ref=part, send_sem=send_sem, recv_sem=recv_sem,
            device_id=(me, up_y), device_id_type=MESH,
        )

    exchange(msg1, recv1, xsem_s.at[0], xsem_r.at[0], False)

    e_hi, e_lo = split2(jnp.exp(cum))
    expcum[...] = mm(e_hi, expand) + mm(e_lo, expand)
    scores = mm_nt(c_ref[...], b_ref[...]) * causal
    low_half = (iota((TOK, 128), 1) < 64).astype(F32)
    skip_wide = small_wide[3:4, :] + small_wide[4:5, :] + small_wide[5:6, :]
    for l in range(8):
        lanes = slice(l * 128, (l + 1) * 128)
        mixes = []
        for h in (2 * l, 2 * l + 1):
            gap = jnp.minimum(cum[:, h : h + 1] - cum_t[h : h + 1, :], 0.0)
            mixes.append((jnp.exp(gap) * scores * dt_t[h : h + 1, :]).astype(BF16))
        x_l = x_wide[:, lanes]
        x_lo = x_l * low_half
        rhs = jnp.concatenate([x_lo.astype(BF16), (x_l - x_lo).astype(BF16)], axis=0)
        ybuf[:, lanes] = mm(jnp.concatenate(mixes, axis=1), rhs) + skip_wide[:, lanes] * x_l
        z_l = z_ref[:, lanes].astype(F32)
        szbuf[:, lanes] = 0.5 * z_l * (1.0 + jnp.tanh(0.5 * z_l))

    routes_t = routes_ref[...]
    rw_t = rw_ref[...]
    dz = ((routes_t >> 3) - zme + 8) & 7
    group = jnp.zeros_like(dz)
    for n, value in enumerate(DZ):
        group = jnp.where(dz == value, n, group)
    off = group * 8 + ((((routes_t >> 1) & 3) - xme + 4) & 3) * 2 + (((routes_t & 1) - cme + 2) & 1)
    place = iota((NS, TOK), 0)
    first = off[0:1, :] == place
    second = off[1:2, :] == place
    named = jnp.where(first, 1.0, 0.0) + jnp.where(second, 1.0, 0.0)
    weight = jnp.where(first, rw_t[0:1, :], 0.0) + jnp.where(second, rw_t[1:2, :], 0.0)
    before = (rows < cols).astype(BF16)
    rank = mm(named.astype(BF16), before)
    rank = jnp.where(named > 0.5, rank, -1.0)
    slot_id = iota((NS, SLOTS, TOK), 1).astype(F32)
    hit = jnp.broadcast_to(rank[:, None, :], (NS, SLOTS, TOK)) == slot_id
    pick = jnp.where(hit, 1.0, 0.0).reshape(NS * SLOTS, TOK).astype(BF16)
    pick_w = jnp.where(hit, jnp.broadcast_to(weight[:, None, :], (NS, SLOTS, TOK)), 0.0).reshape(NS * SLOTS, TOK)
    pw_hi, pw_lo = split2(pick_w)
    wts[0] = mm_nt(eye, pw_hi).astype(BF16)
    wts[1] = mm_nt(eye, pw_lo).astype(BF16)

    loads[0].wait()
    sel16 = (iota((16, 128), 1) == iota((16, 128), 0) + plane * 16).astype(F32)
    state = mm_nt(sel16, init_v[...], HI)
    exchanged(recv1, xsem_s.at[0], xsem_r.at[0]).wait_recv()
    total = jnp.zeros((128, 128), F32)
    decay = jnp.ones((1, 128), F32)
    for j in range(NP):
        inner[j] = total
        through[j : j + 1, :] = decay
        step = recv1[j, 128:144, :].astype(F32)
        step = step[0:1, :] + step[1:2, :] + step[2:3, :]
        total = step * total + recv1[j, 0:128, :].astype(F32)
        decay = step * decay
    r16 = iota((16, 128), 0)
    tail = jnp.zeros((16, 128), F32)
    for n, part in enumerate(split3(decay)):
        tail = jnp.where(r16 == n, part.astype(F32), tail)
    for j in range(NZ):
        msg2[j, 0:16, :] = total[j * 16 : (j + 1) * 16, :].astype(BF16)
        msg2[j, 16:32, :] = tail.astype(BF16)
    exchange(msg2, recv2, xsem_s.at[1], xsem_r.at[1], True)
    exchanged(recv2, xsem_s.at[1], xsem_r.at[1]).wait_recv()
    for j in range(NZ):
        msg3[j] = state.astype(BF16)
        piece = recv2[j].astype(F32)
        state = (piece[16:17, :] + piece[17:18, :] + piece[18:19, :]) * state + piece[0:16, :]
    exchange(msg3, recv3, xsem_s.at[2], xsem_r.at[2], True)
    exchanged(recv3, xsem_s.at[2], xsem_r.at[2]).wait_recv()
    entry = recv3[...].astype(F32).reshape(128, 128)
    for j in range(NP):
        msg4[j] = (through[j : j + 1, :] * entry + inner[j]).astype(BF16)
    exchange(msg4, recv4, xsem_s.at[3], xsem_r.at[3], False)
    exchanged(recv4, xsem_s.at[3], xsem_r.at[3]).wait_recv()

    same_head = (iota((128, 128), 0) // 64 == iota((128, 128), 1) // 64).astype(BF16)
    c_bf = c_ref[...]
    for l in range(8):
        lanes = slice(l * 128, (l + 1) * 128)
        v = ybuf[:, lanes] + mm(c_bf, recv4[l]) * expcum[:, lanes]
        v = v * szbuf[:, lanes]
        mean_sq = mm((v * v).astype(BF16), same_head) * (1.0 / 64.0)
        normed[:, lanes] = (v * lax.rsqrt(mean_sq + 1e-05) * ngain_ref[:, lanes]).astype(BF16)

    def rs_copy(n, k):
        sent, landed, side = (far_s, far_r, k) if k < 2 else (near_s, near_r, k - 2)
        return pltpu.make_async_remote_copy(
            src_ref=sent.at[n, side], dst_ref=landed.at[n, side],
            send_sem=rs_s.at[n, k], recv_sem=rs_r.at[n, k],
            device_id=(me, dn_y if side else up_y), device_id_type=MESH,
        )

    half = GR // 2

    def columns(w_v, where):
        return w_v[:, pl.ds(pl.multiple_of(where * SLICE, SLICE), SLICE)]

    def rs_begin(pair, lhs, w_v):
        part = mm(lhs, columns(w_v, far_y)).astype(BF16)
        for n in (0, 1):
            far_s[2 * pair + n, 0] = part[n * GR : n * GR + half]
            far_s[2 * pair + n, 1] = part[n * GR + half : (n + 1) * GR]
            rs_copy(2 * pair + n, 0).start()
            rs_copy(2 * pair + n, 1).start()
        for slot, where in ((0, up_y), (1, dn_y), (2, y)):
            part = mm(lhs, columns(w_v, where))
            pbuf[2 * pair, slot] = part[:GR]
            pbuf[2 * pair + 1, slot] = part[GR:]

    def rs_middle(n):
        rs_copy(n, 0).wait_recv()
        near_s[n, 0, :half] = (pbuf[n, 0, :half] + far_r[n, 0].astype(F32)).astype(BF16)
        near_s[n, 0, half:] = pbuf[n, 0, half:].astype(BF16)
        rs_copy(n, 2).start()
        rs_copy(n, 1).wait_recv()
        near_s[n, 1, :half] = pbuf[n, 1, :half].astype(BF16)
        near_s[n, 1, half:] = (pbuf[n, 1, half:] + far_r[n, 1].astype(F32)).astype(BF16)
        rs_copy(n, 3).start()

    def rs_end(n):
        rs_copy(n, 2).wait_recv()
        rs_copy(n, 3).wait_recv()
        return pbuf[n, 2] + near_r[n, 0].astype(F32) + near_r[n, 1].astype(F32)

    loads[2].wait()
    rs_begin(PAIRS, normed[...], wout_v)
    loads[1].wait()
    rs_middle(GROUPS)
    rs_middle(GROUPS + 1)
    summed = jnp.concatenate([rs_end(GROUPS), rs_end(GROUPS + 1)], axis=0)
    hidden = (tok_v[...].astype(F32) + summed).astype(BF16)
    hid[...] = hidden
    disp[...] = mm(pick, hidden).astype(BF16).reshape(NS, SLOTS, SLICE)

    def spread(k, sent, landed, send_sem, recv_sem, sign):
        for j in FAR_SPOT:
            if j == 0 and DZ[k] == 0:
                continue
            i = k * NP + j
            dest = z_terms[sign * DZ[k] % NZ] + (spots if sign > 0 else spots_back)[j]
            pltpu.make_async_remote_copy(
                src_ref=sent.at[i], dst_ref=landed.at[i], send_sem=send_sem, recv_sem=recv_sem,
                device_id=(dest, y), device_id_type=MESH,
            ).start()

    def gathered(k, landed, send_sem, recv_sem):
        first = 0 if DZ[k] else 1
        part = landed.at[pl.ds(k * NP + first, NP - first)]
        return pltpu.make_async_remote_copy(
            src_ref=part, dst_ref=part, send_sem=send_sem, recv_sem=recv_sem,
            device_id=(me, up_y), device_id_type=MESH,
        )

    own_x = xs.at[0]
    for k in range(4):
        spread(k, disp, own_x, sd, rd.at[k], 1)
    xs[0, OWN] = disp[OWN]
    for load in loads[3:]:
        load.wait()

    def ag_copy(g, k):
        src, dst, first, count, peer = (
            (0, 1, 0, NP, up_y),
            (0, 3, 0, NP, dn_y),
            (1, 2, 0, NP // 2, up_y),
            (3, 2, NP // 2, NP // 2, dn_y),
        )[k]
        part = pl.ds(g * NP + first, count)
        return pltpu.make_async_remote_copy(
            src_ref=xs.at[src, part], dst_ref=xs.at[dst, part],
            send_sem=ag_s.at[g, k], recv_sem=ag_r.at[g, k], device_id=(me, peer), device_id_type=MESH,
        )

    def arrive(k):
        gathered(k, own_x, sd, rd.at[k]).wait_recv()
        ag_copy(k, 0).start()
        ag_copy(k, 1).start()
        if k + 4 < NZ:
            spread(k + 4, disp, own_x, sd, rd.at[k + 4], 1)

    def forward(g):
        ag_copy(g, 0).wait_recv()
        ag_copy(g, 2).start()
        ag_copy(g, 1).wait_recv()
        ag_copy(g, 3).start()

    def expert(pair):
        for g in (2 * pair, 2 * pair + 1):
            ag_copy(g, 2).wait_recv()
            ag_copy(g, 3).wait_recv()
        accg[...] = jnp.zeros_like(accg)
        accu[...] = jnp.zeros_like(accu)

        def piece(o, total):
            owner = lax.rem(y + NY - o, NY)
            at = pl.multiple_of(owner * SLICE, SLICE)
            v = xs[o, pl.ds(2 * pair * GS, 2 * GS)].astype(F32).reshape(2 * GR, SLICE)
            vg = (v * mgain_ref[:, pl.ds(at, SLICE)]).astype(BF16)
            accg[...] += mm(vg, wg_v[pl.ds(at, SLICE), :])
            accu[...] += mm(vg, wu_v[pl.ds(at, SLICE), :])
            return total + jnp.sum(v * v, axis=1, keepdims=True)

        total = lax.fori_loop(0, NY, piece, jnp.zeros((2 * GR, 1), F32))
        scale = lax.rsqrt(total * (1.0 / WIDTH) + 1e-05)
        gate = accg[...] * scale
        act = (0.5 * gate * (1.0 + jnp.tanh(0.5 * gate)) * (accu[...] * scale)).astype(BF16)
        rs_begin(pair, act, wd_v)

    def give_back(g):
        rets[g * GS : (g + 1) * GS] = rs_end(g).astype(BF16).reshape(GS, SLOTS, SLICE)

        spread(g, rets, retr, sr, rr.at[g], -1)

    arrive(0)
    arrive(1)
    forward(0)
    arrive(2)
    forward(1)
    arrive(3)
    forward(2)
    arrive(4)
    forward(3)
    arrive(5)
    forward(4)
    expert(0)
    arrive(6)
    forward(5)
    arrive(7)
    forward(6)
    expert(1)
    rs_middle(0)
    rs_middle(1)
    forward(7)
    expert(2)
    rs_middle(2)
    rs_middle(3)
    give_back(0)
    give_back(1)
    expert(3)
    rs_middle(4)
    rs_middle(5)
    give_back(2)
    give_back(3)
    rs_middle(6)
    rs_middle(7)
    give_back(4)
    give_back(5)
    give_back(6)
    give_back(7)

    retr[OWN] = rets[OWN]
    total = hid[...].astype(F32)
    for g in range(GROUPS):
        gathered(g, retr, sr, rr.at[g]).wait_recv()
        if g % 2:
            back = retr[(g - 1) * GS : (g + 1) * GS].reshape(2 * GR, SLICE)
            lanes = slice((g - 1) * GR, (g + 1) * GR)
            total = total + mm(wts[0, :, lanes], back) + mm(wts[1, :, lanes], back)
    out_ref[...] = total.astype(BF16)

    for n, buf in enumerate((msg1, msg2, msg3, msg4)):
        exchanged(buf, xsem_s.at[n], xsem_r.at[n]).wait_send()
    for buf, sem in ((disp, sd), (rets, sr)):
        part = buf.at[pl.ds(0, NS - 1)]
        pltpu.make_async_remote_copy(
            src_ref=part, dst_ref=part, send_sem=sem, recv_sem=rd.at[0],
            device_id=(me, up_y), device_id_type=MESH,
        ).wait_send()
    for g in range(NZ):
        for k in range(4):
            ag_copy(g, k).wait_send()
    for n in range(GROUPS + 2):
        for k in range(4):
            rs_copy(n, k).wait_send()


def body(
    tokens, input_heads, z_gate, b_proj, c_proj, step_size, decay_log, skip_gain, init_state, norm_gain,
    out_weight, moe_gain, routes, route_weights, w_gate, w_up, w_down,
):
    vmem = pl.BlockSpec(memory_space=pltpu.VMEM)
    hbm = pl.BlockSpec(memory_space=pl.ANY)
    dma = pltpu.SemaphoreType.DMA
    n = GROUPS + 2
    scratch = [
        pltpu.VMEM((NP, 144, 128), BF16),
        pltpu.VMEM((NP, 144, 128), BF16),
        pltpu.VMEM((NZ, 32, 128), BF16),
        pltpu.VMEM((NZ, 32, 128), BF16),
        pltpu.VMEM((NZ, 16, 128), BF16),
        pltpu.VMEM((NZ, 16, 128), BF16),
        pltpu.VMEM((NP, 128, 128), BF16),
        pltpu.VMEM((NP, 128, 128), BF16),
        pltpu.VMEM((NP, 128, 128), F32),
        pltpu.VMEM((NP, 128), F32),
        pltpu.VMEM((TOK, INNER), F32),
        pltpu.VMEM((TOK, INNER), F32),
        pltpu.VMEM((TOK, INNER), F32),
        pltpu.VMEM((TOK, INNER), BF16),
        pltpu.VMEM((TOK, SLICE), BF16),
        pltpu.VMEM((128, 128), F32),
        pltpu.VMEM((INNER, WIDTH), BF16),
        pltpu.VMEM((WIDTH, SLICE), BF16),
        pltpu.VMEM((WIDTH, SLICE), BF16),
        pltpu.VMEM((SLICE, WIDTH), BF16),
        pltpu.VMEM((NS, SLOTS, SLICE), BF16),
        pltpu.VMEM((NY, NS, SLOTS, SLICE), BF16),
        pltpu.VMEM((2 * GR, SLICE), F32),
        pltpu.VMEM((2 * GR, SLICE), F32),
        pltpu.VMEM((TOK, SLICE), BF16),
        pltpu.VMEM((2, TOK, NS * SLOTS), BF16),
        pltpu.VMEM((n, 2, GR // 2, SLICE), BF16),
        pltpu.VMEM((n, 2, GR // 2, SLICE), BF16),
        pltpu.VMEM((n, 2, GR, SLICE), BF16),
        pltpu.VMEM((n, 2, GR, SLICE), BF16),
        pltpu.VMEM((n, 3, GR, SLICE), F32),
        pltpu.VMEM((NS, SLOTS, SLICE), BF16),
        pltpu.VMEM((NS, SLOTS, SLICE), BF16),
        dma((6,)),
        dma((4,)), dma((4,)),
        dma, dma((NZ,)),
        dma, dma((NZ,)),
        dma((NZ, 4)), dma((NZ, 4)),
        dma((n, 4)), dma((n, 4)),
    ]
    return pl.pallas_call(
        kernel,
        out_shape=jax.ShapeDtypeStruct((TOK, SLICE), BF16),
        in_specs=[vmem] * 11 + [hbm] * 6,
        out_specs=vmem,
        scratch_shapes=scratch,
        name="mixer_moe",
        compiler_params=pltpu.CompilerParams(
            collective_id=0, has_side_effects=True, vmem_limit_bytes=56 * 1024 * 1024
        ),
    )(
        input_heads, z_gate, b_proj, c_proj, step_size.T, decay_log.T, skip_gain.reshape(1, HEADS),
        norm_gain.reshape(1, INNER), moe_gain.reshape(1, WIDTH), routes.T, route_weights.T,
        tokens, init_state.reshape(INNER, 128), out_weight, w_gate[0], w_up[0], w_down[0],
    )


def solution(mesh):
    in_specs = (
        P("seq", None),
        P("seq", "tp"),
        P("seq", "tp"),
        P("seq", None),
        P("seq", None),
        P("seq", "tp"),
        P("seq", "tp"),
        P("tp"),
        P("tp", None, None),
        P("tp"),
        P("tp", None),
        P(),
        P("seq", None),
        P("seq", None),
        P("seq", None, "tp"),
        P("seq", None, "tp"),
        P("seq", "tp", None),
    )
    return jax.shard_map(body, mesh=mesh, in_specs=in_specs, out_specs=P("seq", "tp"), check_vma=False)
```

```python
import functools

import jax
import jax.numpy as jnp
from jax import lax
from jax.experimental import pallas as pl
from jax.experimental.pallas import tpu as pltpu
from jax.sharding import PartitionSpec as P

F32 = jnp.float32
BF16 = jnp.bfloat16
HI = lax.Precision.HIGHEST
MESH = pl.DeviceIdType.MESH
NZ, NX, NC = 8, 4, 2
NS = NZ * NX * NC
NP = NX * NC
NY = 4
TOK = 128
HEADS = 16
INNER = 1024
WIDTH = 2048
SLICE = 512
SLOTS = 8
GROUPS = 8
GS = NS // GROUPS
GR = GS * SLOTS
PAIRS = GROUPS // 2
DZ = (0, 1, 7, 3, 5, 4, 2, 6)
OWN = DZ.index(0) * NP
FAR_Z = (4, 3, 5, 2, 6, 1, 7)
FAR_SPOT = (4, 5, 2, 3, 6, 7, 1, 0)


def iota(shape, dim):
    return lax.broadcasted_iota(jnp.int32, shape, dim)


def mm(a, b):
    return jnp.dot(a, b, preferred_element_type=F32)


def mm_nt(a, b, precision=None):
    return lax.dot_general(a, b, (((1,), (1,)), ((), ())), precision=precision, preferred_element_type=F32)


def split2(v):
    hi = v.astype(BF16)
    return hi, (v - hi.astype(F32)).astype(BF16)


def split3(v):
    hi, mid = split2(v)
    low = (v - hi.astype(F32) - mid.astype(F32)).astype(BF16)
    return hi, mid, low


def kernel(
    x_ref, z_ref, b_ref, c_ref, dt_ref, la_ref, skip_ref, ngain_ref, mgain_ref, routes_ref, rw_ref,
    tokens_hbm, init_hbm, wout_hbm, wg_hbm, wu_hbm, wd_hbm,
    out_ref,
    msg1, recv1, msg2, recv2, msg3, recv3, msg4, recv4, inner, through, ybuf, szbuf, expcum, normed,
    tok_v, init_v, wout_v, wg_v, wu_v, wd_v,
    disp, xs, accg, accu, hid, wts,
    far_s, far_r, near_s, near_r, pbuf, rets, retr,
    wsem, xsem_s, xsem_r, sd, rd, sr, rr, ag_s, ag_r, rs_s, rs_r,
):
    me = lax.axis_index("seq")
    y = lax.axis_index("tp")
    up_y = lax.rem(y + 1, NY)
    dn_y = lax.rem(y + NY - 1, NY)
    far_y = lax.rem(y + 2, NY)

    zme, xme, cme = me // NP, lax.rem(me, NP) // NC, lax.rem(me, NC)
    planes = [lax.rem(zme + n, NZ) for n in range(NZ)]
    z_terms = [z * NP for z in planes]
    x_terms = [lax.rem(xme + n, NX) * NC for n in range(NX)]
    c_terms = [cme, 1 - cme]
    spots = [x_terms[n // NC] + c_terms[n % NC] for n in range(NP)]
    spots_back = [x_terms[-(n // NC) % NX] + c_terms[n % NC] for n in range(NP)]

    barrier = pltpu.get_barrier_semaphore()
    plane, spot = zme, spots[0]
    for peer in [z_terms[n] + spot for n in FAR_Z] + [z_terms[0] + spots[n] for n in FAR_SPOT if n]:
        pl.semaphore_signal(barrier, inc=1, device_id=(peer, y), device_id_type=MESH)
    for peer in (up_y, dn_y):
        pl.semaphore_signal(barrier, inc=1, device_id=(me, peer), device_id_type=MESH)

    own_col = pl.multiple_of(y * SLICE, SLICE)
    tile_row = pl.multiple_of(spot * 128, 128)
    loads = [
        pltpu.make_async_copy(init_hbm.at[pl.ds(tile_row, 128), :], init_v, wsem.at[0]),
        pltpu.make_async_copy(tokens_hbm.at[:, pl.ds(own_col, SLICE)], tok_v, wsem.at[1]),
        pltpu.make_async_copy(wout_hbm, wout_v, wsem.at[2]),
        pltpu.make_async_copy(wg_hbm, wg_v, wsem.at[3]),
        pltpu.make_async_copy(wu_hbm, wu_v, wsem.at[4]),
        pltpu.make_async_copy(wd_hbm, wd_v, wsem.at[5]),
    ]
    for load in loads:
        load.start()

    rows = iota((TOK, TOK), 0)
    cols = iota((TOK, TOK), 1)
    causal = (rows >= cols).astype(F32)
    eye = (rows == cols).astype(BF16)
    eye_f = eye.astype(F32)
    dt_t = dt_ref[...]
    cum_t = mm_nt(la_ref[...], causal, HI)
    cum = mm_nt(eye_f, cum_t, HI)
    dt = mm_nt(eye_f, dt_t, HI)
    end = cum[TOK - 1 : TOK, :]
    expand = (iota((HEADS, INNER), 1) // 64 == iota((HEADS, INNER), 0)).astype(BF16)
    w_hi, w_lo = split2(jnp.exp(end - cum) * dt)
    w_wide = mm(w_hi, expand) + mm(w_lo, expand)
    x_wide = x_ref[...].astype(F32)
    xw = (x_wide * w_wide).astype(BF16)
    d3 = split3(jnp.exp(end))
    k3 = split3(skip_ref[...])
    r8 = iota((8, HEADS), 0)
    small = jnp.zeros((8, HEADS), F32)
    for n, part in enumerate(d3 + k3):
        small = jnp.where(r8 == n, part.astype(F32), small)
    small_wide = mm(small.astype(BF16), expand)
    b_t = mm_nt(eye, b_ref[...]).astype(BF16)
    state_t = mm(b_t, xw)
    small_bf = jnp.concatenate([small_wide, small_wide], axis=0).astype(BF16)
    for l in range(NP):
        lanes = slice(l * 128, (l + 1) * 128)
        msg1[l, 0:128, :] = state_t[:, lanes].astype(BF16)
        msg1[l, 128:144, :] = small_bf[:, lanes]

    pl.semaphore_wait(barrier, NP - 1 + NZ - 1 + 2)

    def exchange(sent, landed, send_sem, recv_sem, across):
        mine = plane if across else spot
        for n in FAR_Z if across else FAR_SPOT:
            if n == 0:
                continue
            other = planes[n] if across else spots[n]
            peer = z_terms[n] + spot if across else z_terms[0] + spots[n]
            pltpu.make_async_remote_copy(
                src_ref=sent.at[other], dst_ref=landed.at[mine],
                send_sem=send_sem, recv_sem=recv_sem, device_id=(peer, y), device_id_type=MESH,
            ).start()
        landed[pl.ds(mine, 1)] = sent[pl.ds(mine, 1)]

    def exchanged(landed, send_sem, recv_sem):
        part = landed.at[pl.ds(0, NP - 1)]
        return pltpu.make_async_remote_copy(
            src_ref=part, dst_ref=part, send_sem=send_sem, recv_sem=recv_sem,
            device_id=(me, up_y), device_id_type=MESH,
        )

    exchange(msg1, recv1, xsem_s.at[0], xsem_r.at[0], False)

    e_hi, e_lo = split2(jnp.exp(cum))
    expcum[...] = mm(e_hi, expand) + mm(e_lo, expand)
    scores = mm_nt(c_ref[...], b_ref[...]) * causal
    low_half = (iota((TOK, 128), 1) < 64).astype(F32)
    skip_wide = small_wide[3:4, :] + small_wide[4:5, :] + small_wide[5:6, :]
    for l in range(8):
        lanes = slice(l * 128, (l + 1) * 128)
        mixes = []
        for h in (2 * l, 2 * l + 1):
            gap = jnp.minimum(cum[:, h : h + 1] - cum_t[h : h + 1, :], 0.0)
            mixes.append((jnp.exp(gap) * scores * dt_t[h : h + 1, :]).astype(BF16))
        x_l = x_wide[:, lanes]
        x_lo = x_l * low_half
        rhs = jnp.concatenate([x_lo.astype(BF16), (x_l - x_lo).astype(BF16)], axis=0)
        ybuf[:, lanes] = mm(jnp.concatenate(mixes, axis=1), rhs) + skip_wide[:, lanes] * x_l
        z_l = z_ref[:, lanes].astype(F32)
        szbuf[:, lanes] = 0.5 * z_l * (1.0 + jnp.tanh(0.5 * z_l))

    routes_t = routes_ref[...]
    rw_t = rw_ref[...]
    dz = ((routes_t >> 3) - zme + 8) & 7
    group = jnp.zeros_like(dz)
    for n, value in enumerate(DZ):
        group = jnp.where(dz == value, n, group)
    off = group * 8 + ((((routes_t >> 1) & 3) - xme + 4) & 3) * 2 + (((routes_t & 1) - cme + 2) & 1)
    place = iota((NS, TOK), 0)
    first = off[0:1, :] == place
    second = off[1:2, :] == place
    named = jnp.where(first, 1.0, 0.0) + jnp.where(second, 1.0, 0.0)
    weight = jnp.where(first, rw_t[0:1, :], 0.0) + jnp.where(second, rw_t[1:2, :], 0.0)
    before = (rows < cols).astype(BF16)
    rank = mm(named.astype(BF16), before)
    rank = jnp.where(named > 0.5, rank, -1.0)
    slot_id = iota((NS, SLOTS, TOK), 1).astype(F32)
    hit = jnp.broadcast_to(rank[:, None, :], (NS, SLOTS, TOK)) == slot_id
    pick = jnp.where(hit, 1.0, 0.0).reshape(NS * SLOTS, TOK).astype(BF16)
    pick_w = jnp.where(hit, jnp.broadcast_to(weight[:, None, :], (NS, SLOTS, TOK)), 0.0).reshape(NS * SLOTS, TOK)
    pw_hi, pw_lo = split2(pick_w)
    wts[0] = mm_nt(eye, pw_hi).astype(BF16)
    wts[1] = mm_nt(eye, pw_lo).astype(BF16)

    loads[0].wait()
    sel16 = (iota((16, 128), 1) == iota((16, 128), 0) + plane * 16).astype(F32)
    state = mm_nt(sel16, init_v[...], HI)
    exchanged(recv1, xsem_s.at[0], xsem_r.at[0]).wait_recv()
    total = jnp.zeros((128, 128), F32)
    decay = jnp.ones((1, 128), F32)
    for j in range(NP):
        inner[j] = total
        through[j : j + 1, :] = decay
        step = recv1[j, 128:144, :].astype(F32)
        step = step[0:1, :] + step[1:2, :] + step[2:3, :]
        total = step * total + recv1[j, 0:128, :].astype(F32)
        decay = step * decay
    r16 = iota((16, 128), 0)
    tail = jnp.zeros((16, 128), F32)
    for n, part in enumerate(split3(decay)):
        tail = jnp.where(r16 == n, part.astype(F32), tail)
    for j in range(NZ):
        msg2[j, 0:16, :] = total[j * 16 : (j + 1) * 16, :].astype(BF16)
        msg2[j, 16:32, :] = tail.astype(BF16)
    exchange(msg2, recv2, xsem_s.at[1], xsem_r.at[1], True)
    exchanged(recv2, xsem_s.at[1], xsem_r.at[1]).wait_recv()
    for j in range(NZ):
        msg3[j] = state.astype(BF16)
        piece = recv2[j].astype(F32)
        state = (piece[16:17, :] + piece[17:18, :] + piece[18:19, :]) * state + piece[0:16, :]
    exchange(msg3, recv3, xsem_s.at[2], xsem_r.at[2], True)
    exchanged(recv3, xsem_s.at[2], xsem_r.at[2]).wait_recv()
    entry = recv3[...].astype(F32).reshape(128, 128)
    for j in range(NP):
        msg4[j] = (through[j : j + 1, :] * entry + inner[j]).astype(BF16)
    exchange(msg4, recv4, xsem_s.at[3], xsem_r.at[3], False)
    exchanged(recv4, xsem_s.at[3], xsem_r.at[3]).wait_recv()

    same_head = (iota((128, 128), 0) // 64 == iota((128, 128), 1) // 64).astype(BF16)
    c_bf = c_ref[...]
    for l in range(8):
        lanes = slice(l * 128, (l + 1) * 128)
        v = ybuf[:, lanes] + mm(c_bf, recv4[l]) * expcum[:, lanes]
        v = v * szbuf[:, lanes]
        mean_sq = mm((v * v).astype(BF16), same_head) * (1.0 / 64.0)
        normed[:, lanes] = (v * lax.rsqrt(mean_sq + 1e-05) * ngain_ref[:, lanes]).astype(BF16)

    def rs_copy(n, k):
        sent, landed, side = (far_s, far_r, k) if k < 2 else (near_s, near_r, k - 2)
        return pltpu.make_async_remote_copy(
            src_ref=sent.at[n, side], dst_ref=landed.at[n, side],
            send_sem=rs_s.at[n, k], recv_sem=rs_r.at[n, k],
            device_id=(me, dn_y if side else up_y), device_id_type=MESH,
        )

    half = GR // 2

    def columns(w_v, where):
        return w_v[:, pl.ds(pl.multiple_of(where * SLICE, SLICE), SLICE)]

    def rs_begin(pair, lhs, w_v):
        part = mm(lhs, columns(w_v, far_y)).astype(BF16)
        for n in (0, 1):
            far_s[2 * pair + n, 0] = part[n * GR : n * GR + half]
            far_s[2 * pair + n, 1] = part[n * GR + half : (n + 1) * GR]
            rs_copy(2 * pair + n, 0).start()
            rs_copy(2 * pair + n, 1).start()
        for slot, where in ((0, up_y), (1, dn_y), (2, y)):
            part = mm(lhs, columns(w_v, where))
            pbuf[2 * pair, slot] = part[:GR]
            pbuf[2 * pair + 1, slot] = part[GR:]

    def rs_middle(n):
        rs_copy(n, 0).wait_recv()
        near_s[n, 0, :half] = (pbuf[n, 0, :half] + far_r[n, 0].astype(F32)).astype(BF16)
        near_s[n, 0, half:] = pbuf[n, 0, half:].astype(BF16)
        rs_copy(n, 2).start()
        rs_copy(n, 1).wait_recv()
        near_s[n, 1, :half] = pbuf[n, 1, :half].astype(BF16)
        near_s[n, 1, half:] = (pbuf[n, 1, half:] + far_r[n, 1].astype(F32)).astype(BF16)
        rs_copy(n, 3).start()

    def rs_end(n):
        rs_copy(n, 2).wait_recv()
        rs_copy(n, 3).wait_recv()
        return pbuf[n, 2] + near_r[n, 0].astype(F32) + near_r[n, 1].astype(F32)

    loads[2].wait()
    rs_begin(PAIRS, normed[...], wout_v)
    loads[1].wait()
    rs_middle(GROUPS)
    rs_middle(GROUPS + 1)
    summed = jnp.concatenate([rs_end(GROUPS), rs_end(GROUPS + 1)], axis=0)
    hidden = (tok_v[...].astype(F32) + summed).astype(BF16)
    hid[...] = hidden
    disp[...] = mm(pick, hidden).astype(BF16).reshape(NS, SLOTS, SLICE)

    def spread(k, sent, landed, send_sem, recv_sem, sign):
        for j in FAR_SPOT:
            if j == 0 and DZ[k] == 0:
                continue
            i = k * NP + j
            dest = z_terms[sign * DZ[k] % NZ] + (spots if sign > 0 else spots_back)[j]
            pltpu.make_async_remote_copy(
                src_ref=sent.at[i], dst_ref=landed.at[i], send_sem=send_sem, recv_sem=recv_sem,
                device_id=(dest, y), device_id_type=MESH,
            ).start()

    def gathered(k, landed, send_sem, recv_sem):
        first = 0 if DZ[k] else 1
        part = landed.at[pl.ds(k * NP + first, NP - first)]
        return pltpu.make_async_remote_copy(
            src_ref=part, dst_ref=part, send_sem=send_sem, recv_sem=recv_sem,
            device_id=(me, up_y), device_id_type=MESH,
        )

    own_x = xs.at[0]
    for k in range(4):
        spread(k, disp, own_x, sd, rd.at[k], 1)
    xs[0, OWN] = disp[OWN]
    for load in loads[3:]:
        load.wait()

    def ag_copy(g, k):
        src, dst, first, count, peer = (
            (0, 1, 0, NP, up_y),
            (0, 3, 0, NP, dn_y),
            (1, 2, 0, NP // 2, up_y),
            (3, 2, NP // 2, NP // 2, dn_y),
        )[k]
        part = pl.ds(g * NP + first, count)
        return pltpu.make_async_remote_copy(
            src_ref=xs.at[src, part], dst_ref=xs.at[dst, part],
            send_sem=ag_s.at[g, k], recv_sem=ag_r.at[g, k], device_id=(me, peer), device_id_type=MESH,
        )

    def arrive(k):
        gathered(k, own_x, sd, rd.at[k]).wait_recv()
        ag_copy(k, 0).start()
        ag_copy(k, 1).start()
        if k + 4 < NZ:
            spread(k + 4, disp, own_x, sd, rd.at[k + 4], 1)

    def forward(g):
        ag_copy(g, 0).wait_recv()
        ag_copy(g, 2).start()
        ag_copy(g, 1).wait_recv()
        ag_copy(g, 3).start()

    def expert(pair):
        for g in (2 * pair, 2 * pair + 1):
            ag_copy(g, 2).wait_recv()
            ag_copy(g, 3).wait_recv()
        accg[...] = jnp.zeros_like(accg)
        accu[...] = jnp.zeros_like(accu)

        def piece(o, total):
            owner = lax.rem(y + NY - o, NY)
            at = pl.multiple_of(owner * SLICE, SLICE)
            v = xs[o, pl.ds(2 * pair * GS, 2 * GS)].astype(F32).reshape(2 * GR, SLICE)
            vg = (v * mgain_ref[:, pl.ds(at, SLICE)]).astype(BF16)
            accg[...] += mm(vg, wg_v[pl.ds(at, SLICE), :])
            accu[...] += mm(vg, wu_v[pl.ds(at, SLICE), :])
            return total + jnp.sum(v * v, axis=1, keepdims=True)

        total = lax.fori_loop(0, NY, piece, jnp.zeros((2 * GR, 1), F32))
        scale = lax.rsqrt(total * (1.0 / WIDTH) + 1e-05)
        gate = accg[...] * scale
        act = (0.5 * gate * (1.0 + jnp.tanh(0.5 * gate)) * (accu[...] * scale)).astype(BF16)
        rs_begin(pair, act, wd_v)

    def give_back(g):
        rets[g * GS : (g + 1) * GS] = rs_end(g).astype(BF16).reshape(GS, SLOTS, SLICE)

        spread(g, rets, retr, sr, rr.at[g], -1)

    arrive(0)
    arrive(1)
    forward(0)
    arrive(2)
    forward(1)
    arrive(3)
    forward(2)
    arrive(4)
    forward(3)
    arrive(5)
    forward(4)
    expert(0)
    arrive(6)
    forward(5)
    arrive(7)
    forward(6)
    expert(1)
    rs_middle(0)
    rs_middle(1)
    forward(7)
    expert(2)
    rs_middle(2)
    rs_middle(3)
    give_back(0)
    give_back(1)
    expert(3)
    rs_middle(4)
    rs_middle(5)
    give_back(2)
    give_back(3)
    rs_middle(6)
    rs_middle(7)
    give_back(4)
    give_back(5)
    give_back(6)
    give_back(7)

    retr[OWN] = rets[OWN]
    total = hid[...].astype(F32)
    for g in range(GROUPS):
        gathered(g, retr, sr, rr.at[g]).wait_recv()
        if g % 2:
            back = retr[(g - 1) * GS : (g + 1) * GS].reshape(2 * GR, SLICE)
            lanes = slice((g - 1) * GR, (g + 1) * GR)
            total = total + mm(wts[0, :, lanes], back) + mm(wts[1, :, lanes], back)
    out_ref[...] = total.astype(BF16)

    for n, buf in enumerate((msg1, msg2, msg3, msg4)):
        exchanged(buf, xsem_s.at[n], xsem_r.at[n]).wait_send()
    for buf, sem in ((disp, sd), (rets, sr)):
        part = buf.at[pl.ds(0, NS - 1)]
        pltpu.make_async_remote_copy(
            src_ref=part, dst_ref=part, send_sem=sem, recv_sem=rd.at[0],
            device_id=(me, up_y), device_id_type=MESH,
        ).wait_send()
    for g in range(NZ):
        for k in range(4):
            ag_copy(g, k).wait_send()
    for n in range(GROUPS + 2):
        for k in range(4):
            rs_copy(n, k).wait_send()


def body(
    tokens, input_heads, z_gate, b_proj, c_proj, step_size, decay_log, skip_gain, init_state, norm_gain,
    out_weight, moe_gain, routes, route_weights, w_gate, w_up, w_down,
):
    vmem = pl.BlockSpec(memory_space=pltpu.VMEM)
    hbm = pl.BlockSpec(memory_space=pl.ANY)
    dma = pltpu.SemaphoreType.DMA
    n = GROUPS + 2
    scratch = [
        pltpu.VMEM((NP, 144, 128), BF16),
        pltpu.VMEM((NP, 144, 128), BF16),
        pltpu.VMEM((NZ, 32, 128), BF16),
        pltpu.VMEM((NZ, 32, 128), BF16),
        pltpu.VMEM((NZ, 16, 128), BF16),
        pltpu.VMEM((NZ, 16, 128), BF16),
        pltpu.VMEM((NP, 128, 128), BF16),
        pltpu.VMEM((NP, 128, 128), BF16),
        pltpu.VMEM((NP, 128, 128), F32),
        pltpu.VMEM((NP, 128), F32),
        pltpu.VMEM((TOK, INNER), F32),
        pltpu.VMEM((TOK, INNER), F32),
        pltpu.VMEM((TOK, INNER), F32),
        pltpu.VMEM((TOK, INNER), BF16),
        pltpu.VMEM((TOK, SLICE), BF16),
        pltpu.VMEM((128, 128), F32),
        pltpu.VMEM((INNER, WIDTH), BF16),
        pltpu.VMEM((WIDTH, SLICE), BF16),
        pltpu.VMEM((WIDTH, SLICE), BF16),
        pltpu.VMEM((SLICE, WIDTH), BF16),
        pltpu.VMEM((NS, SLOTS, SLICE), BF16),
        pltpu.VMEM((NY, NS, SLOTS, SLICE), BF16),
        pltpu.VMEM((2 * GR, SLICE), F32),
        pltpu.VMEM((2 * GR, SLICE), F32),
        pltpu.VMEM((TOK, SLICE), BF16),
        pltpu.VMEM((2, TOK, NS * SLOTS), BF16),
        pltpu.VMEM((n, 2, GR // 2, SLICE), BF16),
        pltpu.VMEM((n, 2, GR // 2, SLICE), BF16),
        pltpu.VMEM((n, 2, GR, SLICE), BF16),
        pltpu.VMEM((n, 2, GR, SLICE), BF16),
        pltpu.VMEM((n, 3, GR, SLICE), F32),
        pltpu.VMEM((NS, SLOTS, SLICE), BF16),
        pltpu.VMEM((NS, SLOTS, SLICE), BF16),
        dma((6,)),
        dma((4,)), dma((4,)),
        dma, dma((NZ,)),
        dma, dma((NZ,)),
        dma((NZ, 4)), dma((NZ, 4)),
        dma((n, 4)), dma((n, 4)),
    ]
    return pl.pallas_call(
        kernel,
        out_shape=jax.ShapeDtypeStruct((TOK, SLICE), BF16),
        in_specs=[vmem] * 11 + [hbm] * 6,
        out_specs=vmem,
        scratch_shapes=scratch,
        name="mixer_moe",
        compiler_params=pltpu.CompilerParams(
            collective_id=0, has_side_effects=True, vmem_limit_bytes=56 * 1024 * 1024
        ),
    )(
        input_heads, z_gate, b_proj, c_proj, step_size.T, decay_log.T, skip_gain.reshape(1, HEADS),
        norm_gain.reshape(1, INNER), moe_gain.reshape(1, WIDTH), routes.T, route_weights.T,
        tokens, init_state.reshape(INNER, 128), out_weight, w_gate[0], w_up[0], w_down[0],
    )


def solution(mesh):
    in_specs = (
        P("seq", None),
        P("seq", "tp"),
        P("seq", "tp"),
        P("seq", None),
        P("seq", None),
        P("seq", "tp"),
        P("seq", "tp"),
        P("tp"),
        P("tp", None, None),
        P("tp"),
        P("tp", None),
        P(),
        P("seq", None),
        P("seq", None),
        P("seq", None, "tp"),
        P("seq", None, "tp"),
        P("seq", "tp", None),
    )
    return jax.shard_map(body, mesh=mesh, in_specs=in_specs, out_specs=P("seq", "tp"), check_vma=False)
```
